32 devices in a mesh: band: 4 (over y, x), cell: 8 (over z, core).
Axes of the slice: x: 2, y: 2, z: 4, core: 2. Of those that a mesh axis runs over, the one named last changes fastest.
Arguments:
- wavefunctions: bfloat16 [512, 28672], P('band', 'cell'), may hold values from -24 to 24
- stiffness: bfloat16 [512, 512], replicated, may hold values from -1 to 2
- cell_scale: float32 [64], P('cell'), may hold values from 0.5 to 1.5
- potential: float32 [64, 512], P('cell'), may hold values from 0 to 1
Outputs:
- rotated: bfloat16 [512, 28672], P('band', 'cell')
The draws below stay inside these ranges and needn't reach their ends.
All inputs are finite; a program needn't handle non-finite values.
Results may differ from the reference program's by a relative error of at most 0.0022.
The reference program's roundings to bfloat16 on the way count: a program that leaves them out, or rounds other values in their place, can miss the bound.
Values may be sent and summed in bfloat16 or wider, within the bound.
A program may use at most 64 MiB of HBM per device.

```python
import math
from functools import partial
import jax
import jax.numpy as jnp
from jax import lax

NB = 512
CN = 512
PLANE = 64
OWN = 448
NCELLS = 64
NODES = 28672


def draw_wavefunctions(key, part):
    key_base, key_order, key_scale = jax.random.split(jax.random.fold_in(key, 11), 3)
    base = jnp.clip(jax.random.normal(key_base, (NB, NODES), jnp.float32), -5.0, 5.0)
    order = jax.random.permutation(key_order, NB)
    mixed = base + 0.6 * base[order]
    scales = jnp.exp(jax.random.uniform(key_scale, (NB, 1), jnp.float32, math.log(0.3), math.log(3.0)))
    return (mixed * scales).astype(jnp.bfloat16)


def draw_stiffness(key, part):
    key_noise, key_diag = jax.random.split(jax.random.fold_in(key, 23), 2)
    noise = jnp.clip(jax.random.normal(key_noise, (CN, CN), jnp.float32), -5.0, 5.0)
    diagonal = jax.random.uniform(key_diag, (CN,), jnp.float32, 1.0, 1.5)
    symmetric = (noise + noise.T) * (0.25 / math.sqrt(2.0 * CN))
    return (symmetric + jnp.diag(diagonal)).astype(jnp.bfloat16)


def shard_levels(own_key, extent, cuts, smallest, high):
    def one(dim, shards_of):
        steps = jax.random.uniform(jax.random.fold_in(jax.random.fold_in(own_key, 6), dim), (shards_of,), jnp.float32, smallest / len(cuts), high / len(cuts))
        return jnp.repeat(jnp.exp(steps), extent[dim] // shards_of).reshape((-1,) + (1,) * (len(extent) - dim - 1))

    loudness = one(*cuts[0])
    for cut in cuts[1:]:
        loudness = loudness * one(*cut)
    return loudness


def setup_inputs(seed: int = 0) -> dict:
    key_of = jax.random.split(jax.random.key(seed), 5)
    wavefunctions = draw_wavefunctions(jax.random.fold_in(key_of[4], 71), 0)
    stiffness = draw_stiffness(jax.random.fold_in(key_of[4], 71), 0)
    cell_scale = jnp.clip(jnp.exp(math.log(1.5) - 1.0986123 * jax.random.uniform(key_of[2], (NCELLS,), jnp.float32) ** shard_levels(key_of[2], (NCELLS,), ((0, 8),), -0.2, 0.2)), 0.5, 1.5)
    potential = jnp.clip(1.0 * jax.random.uniform(key_of[3], (NCELLS, CN), jnp.float32) ** shard_levels(key_of[3], (NCELLS, CN), ((0, 8),), -0.2, 0.2), 0.0, 1.0)
    return dict(wavefunctions=wavefunctions, stiffness=stiffness, cell_scale=cell_scale, potential=potential)


centre = 4.0
half_width = 3.0

def apply_group(group, stiffness, cell_scale, potential):
    band_rows = group.shape[0]
    owned_part = group.reshape(band_rows, NCELLS, OWN)
    top_plane = jnp.roll(owned_part, -1, axis=1)[:, :, :PLANE]
    cell_nodes = jnp.concatenate([owned_part, top_plane], 2).astype(jnp.float32)
    stiff_part = jnp.einsum('bcn,nm->bcm', cell_nodes, stiffness.astype(jnp.float32))
    cell_result = cell_scale[None, :, None] * stiff_part + potential[None] * cell_nodes
    spill = jnp.roll(cell_result[:, :, OWN:], 1, axis=1)
    kept = cell_result[:, :, :OWN]
    kept = jnp.concatenate([kept[:, :, :PLANE] + spill, kept[:, :, PLANE:]], 2)
    return kept.reshape(band_rows, NCELLS * OWN)

def apply_h(field, stiffness, cell_scale, potential):
    groups = field.reshape(-1, 64, field.shape[1])
    result = lax.map(partial(apply_group, stiffness=stiffness, cell_scale=cell_scale, potential=potential), groups)
    return result.reshape(field.shape[0], field.shape[1])

def reference(wavefunctions, stiffness, cell_scale, potential):
    anchor = wavefunctions.astype(jnp.float32)
    degree_one = ((apply_h(wavefunctions, stiffness, cell_scale, potential) - centre * anchor) / half_width).astype(jnp.bfloat16)
    one_wide = degree_one.astype(jnp.float32)
    degree_two = (2.0 * (apply_h(degree_one, stiffness, cell_scale, potential) - centre * one_wide) / half_width - anchor).astype(jnp.bfloat16)
    two_wide = degree_two.astype(jnp.float32)
    degree_three = (2.0 * (apply_h(degree_two, stiffness, cell_scale, potential) - centre * two_wide) / half_width - one_wide).astype(jnp.bfloat16)
    margin = jnp.dot(degree_three.astype(jnp.float32), degree_three.T.astype(jnp.float32), preferred_element_type=jnp.float32) / NODES
    factor = jnp.linalg.cholesky(margin)
    identity = jnp.eye(NB, dtype=jnp.float32)
    inverse = jax.scipy.linalg.solve_triangular(factor, identity, lower=True).astype(jnp.bfloat16)
    return jnp.dot(inverse.astype(jnp.float32), degree_three.astype(jnp.float32), preferred_element_type=jnp.float32).astype(jnp.bfloat16)
```

```python
import functools
import jax
import jax.numpy as jnp
from jax import lax
from jax.experimental import pallas as pl
from jax.experimental.pallas import tpu as pltpu
from jax.sharding import PartitionSpec as P

PLANE = 64
OWN = 448
BLK = 128
PAN = 8
SUB = 32
MESH = pl.DeviceIdType.MESH

centre = 4.0
half_width = 3.0


def shifted(block, axis, distance):
    devices = range(lax.axis_size(axis))
    route = [((i - distance) % len(devices), i) for i in devices]
    return lax.ppermute(block, axis, route)


def apply_h(field, stiffness, cell_scale, potential):
    band_rows = field.shape[0]
    cell_count = field.shape[1] // OWN
    following = shifted(field[:, :PLANE], "cell", -1)
    owned_part = field.reshape(band_rows, cell_count, OWN)
    top_plane = jnp.concatenate([owned_part[:, 1:, :PLANE], following[:, None, :]], 1)
    cell_nodes = jnp.concatenate([owned_part, top_plane], 2)
    stiff_part = jnp.einsum(
        "bcn,nm->bcm", cell_nodes, stiffness, preferred_element_type=jnp.float32
    )
    cell_result = cell_scale[None, :, None] * stiff_part + potential[None] * cell_nodes.astype(
        jnp.float32
    )
    spill = cell_result[:, :, OWN:]
    incoming = shifted(spill[:, -1], "cell", 1)
    spill = jnp.concatenate([incoming[:, None, :], spill[:, :-1]], 1)
    kept = cell_result[:, :, :OWN]
    kept = jnp.concatenate([kept[:, :, :PLANE] + spill, kept[:, :, PLANE:]], 2)
    return kept.reshape(band_rows, cell_count * OWN)


def place(i, j, count):
    if i >= count // 2:
        return (count - 1 - i) * BLK, j * BLK
    return i * BLK, (count - i + j) * BLK


def packed_gram(slices_ref, packed_ref, count):
    for i in range(count):
        row, col = place(count - 1 - i, 0, count)
        width = (count - i) * BLK
        packed_ref[row : row + BLK, col : col + width] = lax.dot_general(
            slices_ref[i * BLK : (i + 1) * BLK, :],
            slices_ref[i * BLK :, :],
            (((1,), (1,)), ((), ())),
            preferred_element_type=jnp.float32,
        )


def gram_kernel(count, slices_ref, packed_ref):
    packed_gram(slices_ref, packed_ref, count)


def rows_at(start, size):
    return pl.ds(pl.multiple_of(start, 8), size)


def pair_step(e, degree, source, older, target, st, potb, potx, shift=0):
    at = lambda c, skip, size: pl.ds(pl.multiple_of(c * OWN + skip, 16), size)
    nodes = OWN + PLANE
    va, vb = source[at(e, 0, nodes), :], source[at(e + 1, 0, nodes), :]
    vp = source[at(e - 1, 0, nodes), :]
    both = jnp.dot(st[...], jnp.concatenate([va, vb], 1), preferred_element_type=jnp.float32)
    before = jnp.dot(st[OWN:nodes, :], vp, preferred_element_type=jnp.float32)
    scale = lambda c: potx[c][:, nodes:]
    wa, wb = va.astype(jnp.float32), vb.astype(jnp.float32)
    ya = scale(e) * both[:, :BLK] + potb[e] * wa
    yb = scale(e + 1) * both[:, BLK:] + potb[e + 1] * wb
    yp = scale(e - 1) * before + potb[e - 1, OWN:, :] * vp[OWN:].astype(jnp.float32)

    def finish(c, h, w, skip):
        size = h.shape[0]
        value = h - centre * w
        if degree == 1:
            value = value * (1.0 / half_width)
        else:
            value = value * (2.0 / half_width) - older[at(c, skip, size), :].astype(jnp.float32)
        target[at(c - shift, skip, size), :] = value.astype(target.dtype)

    finish(e, ya[:PLANE] + yp, wa[:PLANE], 0)
    finish(e, ya[PLANE:OWN], wa[PLANE:OWN], PLANE)
    finish(e + 1, yb[:PLANE] + ya[OWN:], wb[:PLANE], 0)
    finish(e + 1, yb[PLANE:OWN], wb[PLANE:OWN], PLANE)


def send_ahead(turns, bands, band, cell, own_ref, ahead_ref, send_sem, recv_sem, base):
    each = ahead_ref.shape[2]
    wide = len(turns)
    device = lambda b: {"band": b, "cell": cell}

    def copy_to(b, n):
        part = (b + 1 + turns[n]) % bands
        return pltpu.make_async_remote_copy(
            src_ref=own_ref.at[part * each : (part + 1) * each], dst_ref=ahead_ref.at[band, n],
            send_sem=send_sem.at[base + (b - 1) * wide + n], recv_sem=recv_sem.at[base + band * wide + n],
            device_id=device(b), device_id_type=MESH,
        )

    def copy_from(h, n):
        return pltpu.make_async_remote_copy(
            src_ref=own_ref.at[0:each], dst_ref=ahead_ref.at[h, n],
            send_sem=send_sem.at[base + n], recv_sem=recv_sem.at[base + h * wide + n],
            device_id=device(h), device_id_type=MESH,
        )

    for n in range(wide):
        for b in range(1, bands):

            @pl.when(band < b)
            def _():
                copy_to(b, n).start()

    def finish():
        for n in range(wide):
            for b in range(1, bands):

                @pl.when(band < b)
                def _():
                    copy_to(b, n).wait_send()

                @pl.when(b - 1 < band)
                def _():
                    copy_from(b - 1, n).wait_recv()

    return finish


def filter_kernel(
    count, bands, cells, held, total,
    wave_ref, stiff_ref, scale_ref, potential_ref, slices_ref, three, ahead_ref, out_ref,
    pots, turned, ext, one, two, st, potx, potb,
    mine, from_core, half, from_band, quarter, from_z, piece,
    send_sem, recv_sem,
):
    band = lax.axis_index("band")
    cell = lax.axis_index("cell")
    core = lax.rem(cell, 2)
    level = lax.div(cell, 2)
    levels = cells // 2
    rows_half = mine.shape[0] // 2
    rows_band = rows_half // bands
    rows_z = rows_band // levels
    nodes = OWN + PLANE
    owned = held * OWN

    other_core = {"band": band, "cell": cell + 1 - 2 * core}
    band_peer = lambda o: lax.rem(band + o, bands)
    z_peer = lambda o: lax.rem(level + o, levels)
    band_device = lambda o: {"band": band_peer(o), "cell": cell}
    z_device = lambda o: {"band": band, "cell": z_peer(o) * 2 + core}
    cell_device = lambda o: {"band": band, "cell": lax.rem(cell + o, cells)}

    barrier = pltpu.get_barrier_semaphore()
    for o in range(1, bands):
        pl.semaphore_signal(barrier, inc=1, device_id=band_device(o), device_id_type=MESH)
    for o in range(1, cells):
        pl.semaphore_signal(barrier, inc=1, device_id=cell_device(o), device_id_type=MESH)
    used = [0]

    def send(src, dst, device):
        slot = used[0]
        used[0] += 1
        copy = pltpu.make_async_remote_copy(
            src_ref=src, dst_ref=dst, send_sem=send_sem.at[slot], recv_sem=recv_sem.at[slot],
            device_id=device, device_id_type=MESH,
        )
        copy.start()
        return copy

    low, high = 3 * OWN, 2 * OWN + PLANE
    right, left = cell_device(1), cell_device(cells - 1)

    def turn(q):
        span = slice(q * BLK, (q + 1) * BLK)
        turned[span, :] = wave_ref[:, span].T

    strips = owned // BLK
    first, last = -(-high // BLK), (owned - low) // BLK
    for c in range(held):
        pots[c, :, :nodes] = potential_ref[c : c + 1, :]
        pots[c, :, nodes:] = jnp.broadcast_to(scale_ref[:, c : c + 1], (1, BLK))
    for q in range(last, strips):
        turn(q)
    pl.semaphore_wait(barrier, bands - 1 + cells - 1)
    halo = [
        send(pots.at[held - 3 : held], potx.at[0:3], right),
        send(pots.at[0:2], potx.at[held + 3 : held + 5], left),
        send(turned.at[owned - low : owned], ext.at[0:low], right),
    ]
    for q in range(first):
        turn(q)
    halo.append(send(turned.at[0:high], ext.at[low + owned : low + owned + high], left))
    for q in range(first, last):
        turn(q)
    potx[3 : held + 3] = pots[...]
    ext[low : low + owned, :] = turned[...]
    st[...] = stiff_ref[...].T

    def columns(c):
        line = potx[c]
        for q in range(nodes // BLK):
            part = jnp.broadcast_to(line[:, q * BLK : (q + 1) * BLK], (BLK, BLK))
            potb[c, q * BLK : (q + 1) * BLK, :] = part.T

    @pl.loop(3, held + 3)
    def _(c):
        columns(c)

    @pl.loop(0, (held - 4) // 2)
    def _(p):
        pair_step(5 + 2 * p, 1, ext, None, one, st, potb, potx)

    for copy in halo:
        copy.wait()
    for c in (0, 1, 2, held + 3, held + 4):
        columns(c)

    @pl.loop(0, 4)
    def _(p):
        e = jnp.where(p < 2, 1 + 2 * p, held - 3 + 2 * p)
        pair_step(e, 1, ext, None, one, st, potb, potx)

    @pl.loop(0, held // 2 + 1)
    def _(p):
        pair_step(2 + 2 * p, 2, one, ext, two, st, potb, potx)

    each = owned // bands
    pairs = held // 2 // bands
    base = used[0]
    used[0] += bands - 1
    swaps = []
    for o in [*range(1, bands), 0]:
        peer = band_peer(o)

        @pl.loop(0, pairs)
        def _(p):
            pair_step(3 + 2 * (peer * pairs + p), 3, two, one, three, st, potb, potx, 3)

        piece_of = three.at[pl.ds(pl.multiple_of(peer * each, 16), each)]
        if o:
            copy = pltpu.make_async_remote_copy(
                src_ref=piece_of, dst_ref=slices_ref.at[band],
                send_sem=send_sem.at[base + o - 1], recv_sem=recv_sem.at[base + o - 1],
                device_id=band_device(o), device_id_type=MESH,
            )
            copy.start()
            swaps.append(copy)
        else:
            slices_ref[band] = piece_of[...]
    for copy in swaps:
        copy.wait()

    for i in range(count):
        row, col = place(count - 1 - i, 0, count)
        width = (count - i) * BLK
        joined = jnp.concatenate([slices_ref[j] for j in range(i, count)], 1)
        mine[row : row + BLK, col : col + width] = jnp.dot(
            slices_ref[i].T, joined, preferred_element_type=jnp.float32
        )

    cuts = [0, (count + 2) // 2 * BLK, (count + 1) * BLK]
    spans = [slice(cuts[n], cuts[n + 1]) for n in range(2)]
    start_half = core * rows_half
    start_band = start_half + band * rows_band
    start_z = start_band + level * rows_z

    def each_span(stage):
        return [stage(span) for span in spans]

    def wait_all(copies):
        for copy in copies:
            copy.wait()

    over_core = each_span(
        lambda span: [
            send(
                mine.at[rows_at((1 - core) * rows_half, rows_half), span],
                from_core.at[:, span],
                other_core,
            )
        ]
    )
    over_band = []
    for span, copies in zip(spans, over_core):
        wait_all(copies)
        half[:, span] = mine[rows_at(start_half, rows_half), span] + from_core[:, span]
        over_band.append([
            send(
                half.at[rows_at(band_peer(o) * rows_band, rows_band), span],
                from_band.at[o - 1, :, span],
                band_device(o),
            )
            for o in range(1, bands)
        ])
    over_z = []
    for span, copies in zip(spans, over_band):
        wait_all(copies)
        summed = half[rows_at(band * rows_band, rows_band), span]
        for o in range(1, bands):
            summed = summed + from_band[o - 1, :, span]
        quarter[:, span] = summed
        over_z.append([
            send(
                quarter.at[rows_at(z_peer(o) * rows_z, rows_z), span],
                from_z.at[o - 1, :, span],
                z_device(o),
            )
            for o in range(1, levels)
        ])
    finish_ahead = send_ahead(
        range(0, 1), bands, band, cell, three, ahead_ref, send_sem, recv_sem, send_sem.shape[0] - bands + 1
    )
    back_z = []
    for span, copies in zip(spans, over_z):
        wait_all(copies)
        summed = quarter[rows_at(level * rows_z, rows_z), span]
        for o in range(1, levels):
            summed = summed + from_z[o - 1, :, span]
        summed = summed / total
        piece[:, span] = summed
        here = rows_at(start_z, rows_z)
        out_ref[here, span] = summed
        back_z.append([
            send(piece.at[:, span], out_ref.at[here, span], z_device(o)) for o in range(1, levels)
        ])
    back_band = []
    for span, copies in zip(spans, back_z):
        wait_all(copies)
        here = out_ref.at[rows_at(start_band, rows_band), span]
        back_band.append([send(here, here, band_device(o)) for o in range(1, bands)])
    back_core = []
    for span, copies in zip(spans, back_band):
        wait_all(copies)
        here = out_ref.at[rows_at(start_half, rows_half), span]
        back_core.append([send(here, here, other_core)])
    for copies in back_core:
        wait_all(copies)
    finish_ahead()


def filtered(wavefunctions, stiffness, cell_scale, potential):
    bands, cells = lax.axis_size("band"), lax.axis_size("cell")
    band_rows, owned = wavefunctions.shape
    held = owned // OWN
    nodes = OWN + PLANE
    count = band_rows * bands // BLK
    each = owned // bands
    total = float(owned * cells)
    height, width = count * BLK // 2, (count + 1) * BLK
    levels = cells // 2
    rows_half = height // 2
    rows_band = rows_half // bands
    rows_z = rows_band // levels
    sends = 4 + 2 * (bands - 1) + 4 * (1 + (bands - 1) + (levels - 1))
    spans = owned + 5 * OWN + PLANE
    vmem = pl.BlockSpec(memory_space=pltpu.VMEM)
    f32, bf16 = jnp.float32, jnp.bfloat16
    return pl.pallas_call(
        functools.partial(filter_kernel, count, bands, cells, held, total),
        out_shape=(
            jax.ShapeDtypeStruct((bands, each, BLK), bf16),
            jax.ShapeDtypeStruct((owned, BLK), bf16),
            jax.ShapeDtypeStruct((bands - 1, 1, each, BLK), bf16),
            jax.ShapeDtypeStruct((height, width), f32),
        ),
        in_specs=[vmem] * 4,
        out_specs=(vmem,) * 4,
        scratch_shapes=[
            pltpu.VMEM((held, 1, nodes + BLK), f32),
            pltpu.VMEM((owned, BLK), bf16),
            pltpu.VMEM((spans, BLK), bf16),
            pltpu.VMEM((spans, BLK), bf16),
            pltpu.VMEM((spans, BLK), bf16),
            pltpu.VMEM((nodes, nodes), bf16),
            pltpu.VMEM((held + 5, 1, nodes + BLK), f32),
            pltpu.VMEM((held + 5, nodes, BLK), f32),
            pltpu.VMEM((height, width), f32),
            pltpu.VMEM((rows_half, width), f32),
            pltpu.VMEM((rows_half, width), f32),
            pltpu.VMEM((bands - 1, rows_band, width), f32),
            pltpu.VMEM((rows_band, width), f32),
            pltpu.VMEM((levels - 1, rows_z, width), f32),
            pltpu.VMEM((rows_z, width), f32),
            pltpu.SemaphoreType.DMA((sends,)),
            pltpu.SemaphoreType.DMA((sends,)),
        ],
        compiler_params=pltpu.CompilerParams(collective_id=0, has_side_effects=True),
    )(wavefunctions, stiffness, cell_scale[None, :], potential)


def rotate_kernel(bands, inverse_ref, slices_ref, own_ref, first_ref, rest_ref, out_ref):
    band = lax.axis_index("band")
    each = slices_ref.shape[1]
    for g in range(bands):

        @pl.when(band == g)
        def _():
            some = inverse_ref[g * BLK : (g + 1) * BLK, : (g + 1) * BLK]
            for r in range(bands):
                part = (g + r) % bands
                here = slice(part * each, (part + 1) * each)
                lower = lambda h: (
                    slices_ref[h] if r == 0 else first_ref[h, 0] if r == 1 else rest_ref[h, r - 2]
                )
                joined = jnp.concatenate([lower(h) for h in range(g)] + [own_ref[here, :]], 1)
                out_ref[:, here] = lax.dot_general(
                    some, joined, (((1,), (1,)), ((), ())), preferred_element_type=jnp.float32
                ).astype(out_ref.dtype)


def rotated_here(inverse, slices, own, first, rest):
    bands = slices.shape[0]
    vmem = pl.BlockSpec(memory_space=pltpu.VMEM)
    return pl.pallas_call(
        functools.partial(rotate_kernel, bands),
        out_shape=jax.ShapeDtypeStruct(own.shape[::-1], own.dtype),
        in_specs=[vmem] * 5,
        out_specs=vmem,
    )(inverse, slices, own, first, rest)


def fits(band_rows, owned, bands, cells):
    height = band_rows * bands // 2
    return (
        band_rows == BLK
        and owned % OWN == 0
        and bands >= 3
        and cells % 2 == 0
        and cells >= 4
        and owned // OWN >= 4
        and owned // OWN % (2 * bands) == 0
        and height % (16 * bands * (cells // 2)) == 0
    )


def margin_packed(slices):
    bands, cells = lax.axis_size("band"), lax.axis_size("cell")
    band_total, nodes = slices.shape
    count = band_total // BLK
    shape = jax.ShapeDtypeStruct((band_total // 2, (count + 1) * BLK), jnp.float32)
    vmem = pl.BlockSpec(memory_space=pltpu.VMEM)
    partial = pl.pallas_call(
        functools.partial(gram_kernel, count), out_shape=shape, in_specs=[vmem], out_specs=vmem
    )(slices)
    return lax.psum(partial, ("band", "cell")) / float(nodes * bands * cells)


def eliminate(work, k, later):
    groups, tiles = work.shape[1] // BLK, SUB // PAN
    home, offset = k // BLK, k % BLK
    shape = (PAN, BLK)
    lane = lax.broadcasted_iota(jnp.int32, shape, 1)
    row = lax.broadcasted_iota(jnp.int32, shape, 0)
    part = lambda t, q: (slice(k + t * PAN, k + (t + 1) * PAN), slice(q * BLK, (q + 1) * BLK))
    left = [work[part(t, home)] for t in range(tiles)]
    inside = (lane >= offset) & (lane < offset + SUB)
    right = []
    for t in range(tiles):
        unit = jnp.where(lane == row + (offset + t * PAN), 1.0, 0.0)
        right.append(
            [jnp.where(inside, unit, left[t]) if q == home else work[part(t, q)] for q in range(groups)]
        )
    spread = lambda value: jnp.broadcast_to(value, shape)
    lanes = lambda value, c: jnp.take_along_axis(value, jnp.full(shape, c, jnp.int32), axis=1)
    for m in range(tiles):
        c, more = offset + m * PAN, m + 1 < tiles
        here = range(m, tiles)
        cols = {t: [lanes(left[t], c + j) for j in range(PAN)] for t in here}
        grid = [[spread(cols[m][j][i : i + 1, :]) for i in range(j, PAN)] for j in range(PAN)]
        for j in range(PAN):
            scale = lax.rsqrt(grid[j][0])
            factor = {i: grid[j][i - j] * scale for i in range(j + 1, PAN)}
            for q in range(j + 1, PAN):
                grid[q] = [grid[q][i - q] - factor[i] * factor[q] for i in range(q, PAN)]
            head = {t: cols[t][j] * scale for t in here}
            below = jnp.where(row > j, head[m], 0.0)
            pivot = [spread(value[j : j + 1, :]) * scale for value in right[m]]
            right[m] = [
                jnp.where(row == j, p, value - below * p) for p, value in zip(pivot, right[m])
            ]
            if more:
                ahead = spread(left[m][j : j + 1, :]) * scale
                left[m] = left[m] - below * ahead
            for t in here[1:]:
                right[t] = [value - head[t] * p for p, value in zip(pivot, right[t])]
                left[t] = left[t] - head[t] * ahead
            for i in range(j + 1, PAN):
                for t in here:
                    cols[t][i] = cols[t][i] - factor[i] * head[t]
        for q in range(groups):
            work[part(m, q)] = right[m][q]
        for task in later[m::tiles]:
            task()


def split_rows(work, parts, k):
    rest = work[k : k + SUB, :]
    for n in range(3):
        term = rest.astype(jnp.bfloat16)
        parts[n * SUB : (n + 1) * SUB, :] = term
        rest = rest - term.astype(jnp.float32)


def update_below(work, parts, k, first, last):
    size = work.shape[1]
    home, h = k // BLK, first // BLK
    rows, block = slice(first, last), slice(h * BLK, (h + 1) * BLK)
    term = lambda n, span: parts[n * SUB : (n + 1) * SUB, span]
    turned = jnp.concatenate([term(n, block) for n in (0, 1, 2, 0)], 0).T
    turned = turned[first - h * BLK : last - h * BLK]
    mult = jnp.concatenate([turned, turned], 1)
    for low, high in ((0, home + 1), (max(h, home + 1), size // BLK)):
        if low < high:
            span = slice(low * BLK, high * BLK)
            old = work[rows, span]
            if low <= home < high:
                lane = lax.broadcasted_iota(jnp.int32, old.shape, 1) + low * BLK
                old = jnp.where((lane >= k) & (lane < k + SUB), 0.0, old)
            none = jnp.zeros((2 * SUB, (high - low) * BLK), jnp.bfloat16)
            terms = [term(n, span) for n in (0, 0, 0, 1, 2, 1)] + [none]
            work[rows, span] = old - jnp.dot(
                mult, jnp.concatenate(terms, 0), preferred_element_type=jnp.float32
            )


def factor_kernel(
    count, bands, packed_ref, own_ref, out_ref, rest_ref, work, parts, send_sem, recv_sem
):
    band = lax.axis_index("band")
    cell = lax.axis_index("cell")
    barrier = pltpu.get_barrier_semaphore()
    for o in range(1, bands):
        device = {"band": lax.rem(band + o, bands), "cell": cell}
        pl.semaphore_signal(barrier, inc=1, device_id=device, device_id_type=MESH)
    pl.semaphore_wait(barrier, bands - 1)
    finish = send_ahead(
        range(1, bands - 1), bands, band, cell, own_ref, rest_ref, send_sem, recv_sem, 0
    )
    factor_steps(count, packed_ref, out_ref, work, parts)
    finish()


def factor_steps(count, packed_ref, out_ref, work, parts):
    size = count * BLK
    for i in range(count):
        row, col = place(count - 1 - i, 0, count)
        width = (count - i) * BLK
        work[i * BLK : (i + 1) * BLK, i * BLK :] = packed_ref[row : row + BLK, col : col + width]
    later = []
    for k in range(0, size, SUB):
        eliminate(work, k, later)
        half = parts.at[k // SUB % 2]
        if k + SUB < size:
            split_rows(work, half, k)
            update_below(work, half, k, k + SUB, k + 2 * SUB)
        starts = [k + 2 * SUB, *range((k + 2 * SUB) // BLK * BLK + BLK, size, BLK)]
        later = [
            functools.partial(update_below, work, half, k, first, first // BLK * BLK + BLK)
            for first in starts
            if first < size
        ]
    for k in range(0, size, SUB):
        lane = lax.broadcasted_iota(jnp.int32, (SUB, size), 1)
        kept = jnp.where(lane < k + SUB, work[k : k + SUB, :], 0.0)
        out_ref[k : k + SUB, :] = kept.astype(out_ref.dtype)


def inverse_factor(packed):
    size = packed.shape[0] * 2
    count = size // BLK
    vmem = pl.BlockSpec(memory_space=pltpu.VMEM)
    return pl.pallas_call(
        functools.partial(factor_steps, count),
        out_shape=jax.ShapeDtypeStruct((size, size), jnp.bfloat16),
        in_specs=[vmem],
        out_specs=vmem,
        scratch_shapes=[
            pltpu.VMEM((size, size), jnp.float32),
            pltpu.VMEM((2, 3 * SUB, size), jnp.bfloat16),
        ],
    )(packed)


def inverse_and_rest(packed, own):
    bands = lax.axis_size("band")
    size = packed.shape[0] * 2
    count = size // BLK
    each = own.shape[0] // bands
    copies = (bands - 1) * (bands - 2)
    vmem = pl.BlockSpec(memory_space=pltpu.VMEM)
    return pl.pallas_call(
        functools.partial(factor_kernel, count, bands),
        out_shape=(
            jax.ShapeDtypeStruct((size, size), jnp.bfloat16),
            jax.ShapeDtypeStruct((bands - 1, bands - 2, each, BLK), own.dtype),
        ),
        in_specs=[vmem, vmem],
        out_specs=(vmem, vmem),
        scratch_shapes=[
            pltpu.VMEM((size, size), jnp.float32),
            pltpu.VMEM((2, 3 * SUB, size), jnp.bfloat16),
            pltpu.SemaphoreType.DMA((copies,)),
            pltpu.SemaphoreType.DMA((copies,)),
        ],
        compiler_params=pltpu.CompilerParams(collective_id=1, has_side_effects=True),
    )(packed, own)


def shards(wavefunctions, stiffness, cell_scale, potential):
    if fits(*wavefunctions.shape, lax.axis_size("band"), lax.axis_size("cell")):
        slices, own, first, packed = filtered(wavefunctions, stiffness, cell_scale, potential)
        inverse, rest = inverse_and_rest(packed, own)
        return rotated_here(inverse, slices, own, first, rest)
    anchor = wavefunctions.astype(jnp.float32)
    degree_one = (
        (apply_h(wavefunctions, stiffness, cell_scale, potential) - centre * anchor) / half_width
    ).astype(jnp.bfloat16)
    one_wide = degree_one.astype(jnp.float32)
    degree_two = (
        2.0
        * (apply_h(degree_one, stiffness, cell_scale, potential) - centre * one_wide)
        / half_width
        - anchor
    ).astype(jnp.bfloat16)
    two_wide = degree_two.astype(jnp.float32)
    degree_three = (
        2.0
        * (apply_h(degree_two, stiffness, cell_scale, potential) - centre * two_wide)
        / half_width
        - one_wide
    ).astype(jnp.bfloat16)
    slices = lax.all_to_all(degree_three, "band", split_axis=1, concat_axis=0, tiled=True)
    inverse = inverse_factor(margin_packed(slices))
    rotated = jnp.dot(inverse, slices, preferred_element_type=jnp.float32).astype(jnp.bfloat16)
    return lax.all_to_all(rotated, "band", split_axis=0, concat_axis=1, tiled=True)


def solution(mesh):
    in_specs = (P("band", "cell"), P(), P("cell"), P("cell", None))
    out_specs = P("band", "cell")
    return jax.shard_map(shards, mesh=mesh, in_specs=in_specs, out_specs=out_specs, check_vma=False)
```

```python
import functools
import jax
import jax.numpy as jnp
from jax import lax
from jax.experimental import pallas as pl
from jax.experimental.pallas import tpu as pltpu
from jax.sharding import PartitionSpec as P

PLANE = 64
OWN = 448
BLK = 128
PAN = 8
SUB = 32
EARLY = 1
MIDDLE = 3
MESH = pl.DeviceIdType.MESH

centre = 4.0
half_width = 3.0


def shifted(block, axis, distance):
    devices = range(lax.axis_size(axis))
    route = [((i - distance) % len(devices), i) for i in devices]
    return lax.ppermute(block, axis, route)


def apply_h(field, stiffness, cell_scale, potential):
    band_rows = field.shape[0]
    cell_count = field.shape[1] // OWN
    following = shifted(field[:, :PLANE], "cell", -1)
    owned_part = field.reshape(band_rows, cell_count, OWN)
    top_plane = jnp.concatenate([owned_part[:, 1:, :PLANE], following[:, None, :]], 1)
    cell_nodes = jnp.concatenate([owned_part, top_plane], 2)
    stiff_part = jnp.einsum(
        "bcn,nm->bcm", cell_nodes, stiffness, preferred_element_type=jnp.float32
    )
    cell_result = cell_scale[None, :, None] * stiff_part + potential[None] * cell_nodes.astype(
        jnp.float32
    )
    spill = cell_result[:, :, OWN:]
    incoming = shifted(spill[:, -1], "cell", 1)
    spill = jnp.concatenate([incoming[:, None, :], spill[:, :-1]], 1)
    kept = cell_result[:, :, :OWN]
    kept = jnp.concatenate([kept[:, :, :PLANE] + spill, kept[:, :, PLANE:]], 2)
    return kept.reshape(band_rows, cell_count * OWN)


def place(i, j, count):
    if i >= count // 2:
        return (count - 1 - i) * BLK, j * BLK
    return i * BLK, (count - i + j) * BLK


def packed_gram(slices_ref, packed_ref, count):
    for i in range(count):
        row, col = place(count - 1 - i, 0, count)
        width = (count - i) * BLK
        packed_ref[row : row + BLK, col : col + width] = lax.dot_general(
            slices_ref[i * BLK : (i + 1) * BLK, :],
            slices_ref[i * BLK :, :],
            (((1,), (1,)), ((), ())),
            preferred_element_type=jnp.float32,
        )


def gram_kernel(count, slices_ref, packed_ref):
    packed_gram(slices_ref, packed_ref, count)


def rows_at(start, size):
    return pl.ds(pl.multiple_of(start, 8), size)


def pair_step(e, degree, source, older, target, st, potb, potx, shift=0):
    at = lambda c, skip, size: pl.ds(pl.multiple_of(c * OWN + skip, 16), size)
    nodes = OWN + PLANE
    va, vb = source[at(e, 0, nodes), :], source[at(e + 1, 0, nodes), :]
    vp = source[at(e - 1, 0, nodes), :]
    both = jnp.dot(st[...], jnp.concatenate([va, vb], 1), preferred_element_type=jnp.float32)
    before = jnp.dot(st[OWN:nodes, :], vp, preferred_element_type=jnp.float32)
    scale = lambda c: potx[c][:, nodes:]
    wa, wb = va.astype(jnp.float32), vb.astype(jnp.float32)
    ya = scale(e) * both[:, :BLK] + potb[e] * wa
    yb = scale(e + 1) * both[:, BLK:] + potb[e + 1] * wb
    yp = scale(e - 1) * before + potb[e - 1, OWN:, :] * vp[OWN:].astype(jnp.float32)

    def finish(c, h, w, skip):
        size = h.shape[0]
        value = h - centre * w
        if degree == 1:
            value = value * (1.0 / half_width)
        else:
            value = value * (2.0 / half_width) - older[at(c, skip, size), :].astype(jnp.float32)
        target[at(c - shift, skip, size), :] = value.astype(target.dtype)

    finish(e, ya[:PLANE] + yp, wa[:PLANE], 0)
    finish(e, ya[PLANE:OWN], wa[PLANE:OWN], PLANE)
    finish(e + 1, yb[:PLANE] + ya[OWN:], wb[:PLANE], 0)
    finish(e + 1, yb[PLANE:OWN], wb[PLANE:OWN], PLANE)


def ahead_plan(bands):
    far = lambda i, j: bin(i ^ j).count("1") if bands == 4 else int(i != j)
    turns = {}
    plan = []
    for b in range(1, bands):
        for h in range(b):
            for q in [*range(b), *range(b + 1, bands)]:
                source = min((h, q), key=lambda i: (far(i, b), i != q))
                plan.append((far(source, b), source, b, h, q))
    ordered = []
    for _, source, b, h, q in sorted(plan):
        for part in range(2):
            turn = turns.get((source, b), 0)
            turns[source, b] = turn + 1
            ordered.append((turn, source, b, h, q, part))
    return sorted(ordered)


class Ahead:
    def __init__(self, bands, band, cell, slices, own, target, send_sem, recv_sem):
        self.band, self.bands = band, bands
        self.cell, self.slices, self.own, self.target = cell, slices, own, target
        self.send_sem, self.recv_sem = send_sem, recv_sem
        self.started, self.plan = [], ahead_plan(bands)
        self.count = [0] * bands

    def copy(self, slot, b, h, q, part, held):
        each = self.slices.shape[1]
        size = each // 2
        n = q - (q > b)
        span = pl.ds(part * size, size)
        source = self.slices.at[h, span] if held else self.own.at[pl.ds(q * each + part * size, size)]
        return pltpu.make_async_remote_copy(
            src_ref=source, dst_ref=self.target.at[h, n, span],
            send_sem=self.send_sem.at[slot],
            recv_sem=self.recv_sem.at[(h * (self.bands - 1) + n) * 2 + part],
            device_id={"band": b, "cell": self.cell}, device_id_type=MESH,
        )

    def start(self, first, last):
        for turn, source, b, h, q, part in self.plan:
            if first <= turn < last:
                slot = self.count[source]
                self.count[source] += 1
                copy = self.copy(slot, b, h, q, part, source == q)

                @pl.when(self.band == source)
                def _():
                    copy.start()

                self.started.append((source, b, copy))

    def finish(self):
        for source, b, copy in self.started:

            @pl.when(self.band == source)
            def _():
                copy.wait_send()

            @pl.when(self.band == b)
            def _():
                copy.wait_recv()


def filter_kernel(
    count, bands, cells, held, total,
    wave_ref, stiff_ref, scale_ref, potential_ref, slices_ref, three, ahead_ref, inverse_ref,
    pots, turned, ext, one, two, st, potx, potb,
    mine, from_core, half, from_band, quarter, from_z, piece, out_ref, work, parts,
    send_sem, recv_sem, ahead_send, ahead_recv,
):
    band = lax.axis_index("band")
    cell = lax.axis_index("cell")
    core = lax.rem(cell, 2)
    level = lax.div(cell, 2)
    levels = cells // 2
    rows_half = mine.shape[0] // 2
    rows_band = rows_half // bands
    rows_z = rows_band // levels
    nodes = OWN + PLANE
    owned = held * OWN

    other_core = {"band": band, "cell": cell + 1 - 2 * core}
    band_peer = lambda o: lax.rem(band + o, bands)
    z_peer = lambda o: lax.rem(level + o, levels)
    band_device = lambda o: {"band": band_peer(o), "cell": cell}
    z_device = lambda o: {"band": band, "cell": z_peer(o) * 2 + core}
    cell_device = lambda o: {"band": band, "cell": lax.rem(cell + o, cells)}

    barrier = pltpu.get_barrier_semaphore()
    for o in range(1, bands):
        pl.semaphore_signal(barrier, inc=1, device_id=band_device(o), device_id_type=MESH)
    for o in range(1, cells):
        pl.semaphore_signal(barrier, inc=1, device_id=cell_device(o), device_id_type=MESH)
    used = [0]

    def send(src, dst, device):
        slot = used[0]
        used[0] += 1
        copy = pltpu.make_async_remote_copy(
            src_ref=src, dst_ref=dst, send_sem=send_sem.at[slot], recv_sem=recv_sem.at[slot],
            device_id=device, device_id_type=MESH,
        )
        copy.start()
        return copy

    low, high = 3 * OWN, 2 * OWN + PLANE
    right, left = cell_device(1), cell_device(cells - 1)

    def turn(q):
        span = slice(q * BLK, (q + 1) * BLK)
        turned[span, :] = wave_ref[:, span].T

    strips = owned // BLK
    first, last = -(-high // BLK), (owned - low) // BLK
    for c in range(held):
        pots[c, :, :nodes] = potential_ref[c : c + 1, :]
        pots[c, :, nodes:] = jnp.broadcast_to(scale_ref[:, c : c + 1], (1, BLK))
    for q in range(last, strips):
        turn(q)
    pl.semaphore_wait(barrier, bands - 1 + cells - 1)
    halo = [
        send(pots.at[held - 3 : held], potx.at[0:3], right),
        send(pots.at[0:2], potx.at[held + 3 : held + 5], left),
        send(turned.at[owned - low : owned], ext.at[0:low], right),
    ]
    for q in range(first):
        turn(q)
    halo.append(send(turned.at[0:high], ext.at[low + owned : low + owned + high], left))
    for q in range(first, last):
        turn(q)
    potx[3 : held + 3] = pots[...]
    ext[low : low + owned, :] = turned[...]
    st[...] = stiff_ref[...].T

    def columns(c):
        line = potx[c]
        for q in range(nodes // BLK):
            part = jnp.broadcast_to(line[:, q * BLK : (q + 1) * BLK], (BLK, BLK))
            potb[c, q * BLK : (q + 1) * BLK, :] = part.T

    @pl.loop(3, held + 3)
    def _(c):
        columns(c)

    @pl.loop(0, (held - 4) // 2)
    def _(p):
        pair_step(5 + 2 * p, 1, ext, None, one, st, potb, potx)

    for copy in halo:
        copy.wait()
    for c in (0, 1, 2, held + 3, held + 4):
        columns(c)

    @pl.loop(0, 4)
    def _(p):
        e = jnp.where(p < 2, 1 + 2 * p, held - 3 + 2 * p)
        pair_step(e, 1, ext, None, one, st, potb, potx)

    @pl.loop(0, held // 2 + 1)
    def _(p):
        pair_step(2 + 2 * p, 2, one, ext, two, st, potb, potx)

    each = owned // bands
    pairs = held // 2 // bands
    base = used[0]
    used[0] += bands - 1
    swaps = []
    for o in [*range(1, bands), 0]:
        peer = band_peer(o)

        @pl.loop(0, pairs)
        def _(p):
            pair_step(3 + 2 * (peer * pairs + p), 3, two, one, three, st, potb, potx, 3)

        piece_of = three.at[pl.ds(pl.multiple_of(peer * each, 16), each)]
        if o:
            copy = pltpu.make_async_remote_copy(
                src_ref=piece_of, dst_ref=slices_ref.at[band],
                send_sem=send_sem.at[base + o - 1], recv_sem=recv_sem.at[base + o - 1],
                device_id=band_device(o), device_id_type=MESH,
            )
            copy.start()
            swaps.append(copy)
        else:
            slices_ref[band] = piece_of[...]
    for copy in swaps:
        copy.wait()
    ahead = Ahead(bands, band, cell, slices_ref, three, ahead_ref, ahead_send, ahead_recv)
    ahead.start(0, EARLY)

    for i in range(count):
        row, col = place(count - 1 - i, 0, count)
        width = (count - i) * BLK
        joined = jnp.concatenate([slices_ref[j] for j in range(i, count)], 1)
        mine[row : row + BLK, col : col + width] = jnp.dot(
            slices_ref[i].T, joined, preferred_element_type=jnp.float32
        )

    cuts = [0, (count + 2) // 2 * BLK, (count + 1) * BLK]
    spans = [slice(cuts[n], cuts[n + 1]) for n in range(2)]
    start_half = core * rows_half
    start_band = start_half + band * rows_band
    start_z = start_band + level * rows_z

    def each_span(stage):
        return [stage(span) for span in spans]

    def wait_all(copies):
        for copy in copies:
            copy.wait()

    over_core = each_span(
        lambda span: [
            send(
                mine.at[rows_at((1 - core) * rows_half, rows_half), span],
                from_core.at[:, span],
                other_core,
            )
        ]
    )
    over_band = []
    for span, copies in zip(spans, over_core):
        wait_all(copies)
        half[:, span] = mine[rows_at(start_half, rows_half), span] + from_core[:, span]
        over_band.append([
            send(
                half.at[rows_at(band_peer(o) * rows_band, rows_band), span],
                from_band.at[o - 1, :, span],
                band_device(o),
            )
            for o in range(1, bands)
        ])
    over_z = []
    for span, copies in zip(spans, over_band):
        wait_all(copies)
        summed = half[rows_at(band * rows_band, rows_band), span]
        for o in range(1, bands):
            summed = summed + from_band[o - 1, :, span]
        quarter[:, span] = summed
        over_z.append([
            send(
                quarter.at[rows_at(z_peer(o) * rows_z, rows_z), span],
                from_z.at[o - 1, :, span],
                z_device(o),
            )
            for o in range(1, levels)
        ])
    ahead.start(EARLY, EARLY + MIDDLE)
    back_z = []
    for span, copies in zip(spans, over_z):
        wait_all(copies)
        summed = quarter[rows_at(level * rows_z, rows_z), span]
        for o in range(1, levels):
            summed = summed + from_z[o - 1, :, span]
        summed = summed / total
        piece[:, span] = summed
        here = rows_at(start_z, rows_z)
        out_ref[here, span] = summed
        back_z.append([
            send(piece.at[:, span], out_ref.at[here, span], z_device(o)) for o in range(1, levels)
        ])
    back_band = []
    for span, copies in zip(spans, back_z):
        wait_all(copies)
        here = out_ref.at[rows_at(start_band, rows_band), span]
        back_band.append([send(here, here, band_device(o)) for o in range(1, bands)])
    back_core = []
    for span, copies in zip(spans, back_band):
        wait_all(copies)
        here = out_ref.at[rows_at(start_half, rows_half), span]
        back_core.append([send(here, here, other_core)])
    for copies in back_core:
        wait_all(copies)
    ahead.start(EARLY + MIDDLE, 1 << 10)
    factor_steps(count, out_ref, inverse_ref, work, parts)
    ahead.finish()


def filtered(wavefunctions, stiffness, cell_scale, potential):
    bands, cells = lax.axis_size("band"), lax.axis_size("cell")
    band_rows, owned = wavefunctions.shape
    held = owned // OWN
    nodes = OWN + PLANE
    count = band_rows * bands // BLK
    each = owned // bands
    total = float(owned * cells)
    height, width = count * BLK // 2, (count + 1) * BLK
    levels = cells // 2
    rows_half = height // 2
    rows_band = rows_half // bands
    rows_z = rows_band // levels
    sends = 4 + (bands - 1) + 4 * (1 + (bands - 1) + (levels - 1))
    size = count * BLK
    plan = ahead_plan(bands)
    departs = max(sum(copy[1] == b for copy in plan) for b in range(bands))
    spans = owned + 5 * OWN + PLANE
    vmem = pl.BlockSpec(memory_space=pltpu.VMEM)
    f32, bf16 = jnp.float32, jnp.bfloat16
    return pl.pallas_call(
        functools.partial(filter_kernel, count, bands, cells, held, total),
        out_shape=(
            jax.ShapeDtypeStruct((bands, each, BLK), bf16),
            jax.ShapeDtypeStruct((owned, BLK), bf16),
            jax.ShapeDtypeStruct((bands - 1, bands - 1, each, BLK), bf16),
            jax.ShapeDtypeStruct((size, size), bf16),
        ),
        in_specs=[vmem] * 4,
        out_specs=(vmem,) * 4,
        scratch_shapes=[
            pltpu.VMEM((held, 1, nodes + BLK), f32),
            pltpu.VMEM((owned, BLK), bf16),
            pltpu.VMEM((spans, BLK), bf16),
            pltpu.VMEM((spans, BLK), bf16),
            pltpu.VMEM((spans, BLK), bf16),
            pltpu.VMEM((nodes, nodes), bf16),
            pltpu.VMEM((held + 5, 1, nodes + BLK), f32),
            pltpu.VMEM((held + 5, nodes, BLK), f32),
            pltpu.VMEM((height, width), f32),
            pltpu.VMEM((rows_half, width), f32),
            pltpu.VMEM((rows_half, width), f32),
            pltpu.VMEM((bands - 1, rows_band, width), f32),
            pltpu.VMEM((rows_band, width), f32),
            pltpu.VMEM((levels - 1, rows_z, width), f32),
            pltpu.VMEM((rows_z, width), f32),
            pltpu.VMEM((height, width), f32),
            pltpu.VMEM((size, size), f32),
            pltpu.VMEM((2, 3 * SUB, size), bf16),
            pltpu.SemaphoreType.DMA((sends,)),
            pltpu.SemaphoreType.DMA((sends,)),
            pltpu.SemaphoreType.DMA((departs,)),
            pltpu.SemaphoreType.DMA((2 * (bands - 1) ** 2,)),
        ],
        compiler_params=pltpu.CompilerParams(collective_id=0, has_side_effects=True),
    )(wavefunctions, stiffness, cell_scale[None, :], potential)


def rotate_kernel(bands, inverse_ref, slices_ref, own_ref, ahead_ref, out_ref):
    band = lax.axis_index("band")
    each = slices_ref.shape[1]
    for g in range(bands):

        @pl.when(band == g)
        def _():
            some = inverse_ref[g * BLK : (g + 1) * BLK, : (g + 1) * BLK]
            for part in range(bands):
                here = slice(part * each, (part + 1) * each)
                lower = lambda h: slices_ref[h] if part == g else ahead_ref[h, part - (part > g)]
                joined = jnp.concatenate([lower(h) for h in range(g)] + [own_ref[here, :]], 1)
                out_ref[:, here] = lax.dot_general(
                    some, joined, (((1,), (1,)), ((), ())), preferred_element_type=jnp.float32
                ).astype(out_ref.dtype)


def rotated_here(inverse, slices, own, ahead):
    bands = slices.shape[0]
    vmem = pl.BlockSpec(memory_space=pltpu.VMEM)
    return pl.pallas_call(
        functools.partial(rotate_kernel, bands),
        out_shape=jax.ShapeDtypeStruct(own.shape[::-1], own.dtype),
        in_specs=[vmem] * 4,
        out_specs=vmem,
    )(inverse, slices, own, ahead)


def fits(band_rows, owned, bands, cells):
    height = band_rows * bands // 2
    return (
        band_rows == BLK
        and owned % OWN == 0
        and bands >= 3
        and cells % 2 == 0
        and cells >= 4
        and owned // OWN >= 4
        and owned // OWN % (2 * bands) == 0
        and height % (16 * bands * (cells // 2)) == 0
    )


def margin_packed(slices):
    bands, cells = lax.axis_size("band"), lax.axis_size("cell")
    band_total, nodes = slices.shape
    count = band_total // BLK
    shape = jax.ShapeDtypeStruct((band_total // 2, (count + 1) * BLK), jnp.float32)
    vmem = pl.BlockSpec(memory_space=pltpu.VMEM)
    partial = pl.pallas_call(
        functools.partial(gram_kernel, count), out_shape=shape, in_specs=[vmem], out_specs=vmem
    )(slices)
    return lax.psum(partial, ("band", "cell")) / float(nodes * bands * cells)


def eliminate(work, k, later):
    groups, tiles = work.shape[1] // BLK, SUB // PAN
    home, offset = k // BLK, k % BLK
    shape = (PAN, BLK)
    lane = lax.broadcasted_iota(jnp.int32, shape, 1)
    row = lax.broadcasted_iota(jnp.int32, shape, 0)
    part = lambda t, q: (slice(k + t * PAN, k + (t + 1) * PAN), slice(q * BLK, (q + 1) * BLK))
    left = [work[part(t, home)] for t in range(tiles)]
    inside = (lane >= offset) & (lane < offset + SUB)
    right = []
    for t in range(tiles):
        unit = jnp.where(lane == row + (offset + t * PAN), 1.0, 0.0)
        right.append(
            [jnp.where(inside, unit, left[t]) if q == home else work[part(t, q)] for q in range(groups)]
        )
    spread = lambda value: jnp.broadcast_to(value, shape)
    lanes = lambda value, c: jnp.take_along_axis(value, jnp.full(shape, c, jnp.int32), axis=1)
    for m in range(tiles):
        c, more = offset + m * PAN, m + 1 < tiles
        here = range(m, tiles)
        cols = {t: [lanes(left[t], c + j) for j in range(PAN)] for t in here}
        grid = [[spread(cols[m][j][i : i + 1, :]) for i in range(j, PAN)] for j in range(PAN)]
        for j in range(PAN):
            scale = lax.rsqrt(grid[j][0])
            factor = {i: grid[j][i - j] * scale for i in range(j + 1, PAN)}
            for q in range(j + 1, PAN):
                grid[q] = [grid[q][i - q] - factor[i] * factor[q] for i in range(q, PAN)]
            head = {t: cols[t][j] * scale for t in here}
            below = jnp.where(row > j, head[m], 0.0)
            pivot = [spread(value[j : j + 1, :]) * scale for value in right[m]]
            right[m] = [
                jnp.where(row == j, p, value - below * p) for p, value in zip(pivot, right[m])
            ]
            if more:
                ahead = spread(left[m][j : j + 1, :]) * scale
                left[m] = left[m] - below * ahead
            for t in here[1:]:
                right[t] = [value - head[t] * p for p, value in zip(pivot, right[t])]
                left[t] = left[t] - head[t] * ahead
            for i in range(j + 1, PAN):
                for t in here:
                    cols[t][i] = cols[t][i] - factor[i] * head[t]
        for q in range(groups):
            work[part(m, q)] = right[m][q]
        for task in later[m::tiles]:
            task()


def split_rows(work, parts, k):
    rest = work[k : k + SUB, :]
    for n in range(3):
        term = rest.astype(jnp.bfloat16)
        parts[n * SUB : (n + 1) * SUB, :] = term
        rest = rest - term.astype(jnp.float32)


def update_below(work, parts, k, first, last):
    size = work.shape[1]
    home, h = k // BLK, first // BLK
    rows, block = slice(first, last), slice(h * BLK, (h + 1) * BLK)
    term = lambda n, span: parts[n * SUB : (n + 1) * SUB, span]
    turned = jnp.concatenate([term(n, block) for n in (0, 1, 2, 0)], 0).T
    turned = turned[first - h * BLK : last - h * BLK]
    mult = jnp.concatenate([turned, turned], 1)
    for low, high in ((0, home + 1), (max(h, home + 1), size // BLK)):
        if low < high:
            span = slice(low * BLK, high * BLK)
            old = work[rows, span]
            if low <= home < high:
                lane = lax.broadcasted_iota(jnp.int32, old.shape, 1) + low * BLK
                old = jnp.where((lane >= k) & (lane < k + SUB), 0.0, old)
            none = jnp.zeros((2 * SUB, (high - low) * BLK), jnp.bfloat16)
            terms = [term(n, span) for n in (0, 0, 0, 1, 2, 1)] + [none]
            work[rows, span] = old - jnp.dot(
                mult, jnp.concatenate(terms, 0), preferred_element_type=jnp.float32
            )


def factor_steps(count, packed_ref, out_ref, work, parts):
    size = count * BLK
    for i in range(count):
        row, col = place(count - 1 - i, 0, count)
        width = (count - i) * BLK
        work[i * BLK : (i + 1) * BLK, i * BLK :] = packed_ref[row : row + BLK, col : col + width]
    later = []
    for k in range(0, size, SUB):
        eliminate(work, k, later)
        half = parts.at[k // SUB % 2]
        if k + SUB < size:
            split_rows(work, half, k)
            update_below(work, half, k, k + SUB, k + 2 * SUB)
        starts = [k + 2 * SUB, *range((k + 2 * SUB) // BLK * BLK + BLK, size, BLK)]
        later = [
            functools.partial(update_below, work, half, k, first, first // BLK * BLK + BLK)
            for first in starts
            if first < size
        ]
    for k in range(0, size, SUB):
        lane = lax.broadcasted_iota(jnp.int32, (SUB, size), 1)
        kept = jnp.where(lane < k + SUB, work[k : k + SUB, :], 0.0)
        out_ref[k : k + SUB, :] = kept.astype(out_ref.dtype)


def inverse_factor(packed):
    size = packed.shape[0] * 2
    count = size // BLK
    vmem = pl.BlockSpec(memory_space=pltpu.VMEM)
    return pl.pallas_call(
        functools.partial(factor_steps, count),
        out_shape=jax.ShapeDtypeStruct((size, size), jnp.bfloat16),
        in_specs=[vmem],
        out_specs=vmem,
        scratch_shapes=[
            pltpu.VMEM((size, size), jnp.float32),
            pltpu.VMEM((2, 3 * SUB, size), jnp.bfloat16),
        ],
    )(packed)


def shards(wavefunctions, stiffness, cell_scale, potential):
    if fits(*wavefunctions.shape, lax.axis_size("band"), lax.axis_size("cell")):
        slices, own, ahead, inverse = filtered(wavefunctions, stiffness, cell_scale, potential)
        return rotated_here(inverse, slices, own, ahead)
    anchor = wavefunctions.astype(jnp.float32)
    degree_one = (
        (apply_h(wavefunctions, stiffness, cell_scale, potential) - centre * anchor) / half_width
    ).astype(jnp.bfloat16)
    one_wide = degree_one.astype(jnp.float32)
    degree_two = (
        2.0
        * (apply_h(degree_one, stiffness, cell_scale, potential) - centre * one_wide)
        / half_width
        - anchor
    ).astype(jnp.bfloat16)
    two_wide = degree_two.astype(jnp.float32)
    degree_three = (
        2.0
        * (apply_h(degree_two, stiffness, cell_scale, potential) - centre * two_wide)
        / half_width
        - one_wide
    ).astype(jnp.bfloat16)
    slices = lax.all_to_all(degree_three, "band", split_axis=1, concat_axis=0, tiled=True)
    inverse = inverse_factor(margin_packed(slices))
    rotated = jnp.dot(inverse, slices, preferred_element_type=jnp.float32).astype(jnp.bfloat16)
    return lax.all_to_all(rotated, "band", split_axis=0, concat_axis=1, tiled=True)


def solution(mesh):
    in_specs = (P("band", "cell"), P(), P("cell"), P("cell", None))
    out_specs = P("band", "cell")
    return jax.shard_map(shards, mesh=mesh, in_specs=in_specs, out_specs=out_specs, check_vma=False)
```

```python
import functools
import jax
import jax.numpy as jnp
from jax import lax
from jax.experimental import pallas as pl
from jax.experimental.pallas import tpu as pltpu
from jax.sharding import PartitionSpec as P

PLANE = 64
OWN = 448
BLK = 128
PAN = 8
SUB = 32
EARLY = 1
MIDDLE = 3
MESH = pl.DeviceIdType.MESH

centre = 4.0
half_width = 3.0


def shifted(block, axis, distance):
    devices = range(lax.axis_size(axis))
    route = [((i - distance) % len(devices), i) for i in devices]
    return lax.ppermute(block, axis, route)


def apply_h(field, stiffness, cell_scale, potential):
    band_rows = field.shape[0]
    cell_count = field.shape[1] // OWN
    following = shifted(field[:, :PLANE], "cell", -1)
    owned_part = field.reshape(band_rows, cell_count, OWN)
    top_plane = jnp.concatenate([owned_part[:, 1:, :PLANE], following[:, None, :]], 1)
    cell_nodes = jnp.concatenate([owned_part, top_plane], 2)
    stiff_part = jnp.einsum(
        "bcn,nm->bcm", cell_nodes, stiffness, preferred_element_type=jnp.float32
    )
    cell_result = cell_scale[None, :, None] * stiff_part + potential[None] * cell_nodes.astype(
        jnp.float32
    )
    spill = cell_result[:, :, OWN:]
    incoming = shifted(spill[:, -1], "cell", 1)
    spill = jnp.concatenate([incoming[:, None, :], spill[:, :-1]], 1)
    kept = cell_result[:, :, :OWN]
    kept = jnp.concatenate([kept[:, :, :PLANE] + spill, kept[:, :, PLANE:]], 2)
    return kept.reshape(band_rows, cell_count * OWN)


def place(i, j, count):
    if i >= count // 2:
        return (count - 1 - i) * BLK, j * BLK
    return i * BLK, (count - i + j) * BLK


def packed_gram(slices_ref, packed_ref, count):
    for i in range(count):
        row, col = place(count - 1 - i, 0, count)
        width = (count - i) * BLK
        packed_ref[row : row + BLK, col : col + width] = lax.dot_general(
            slices_ref[i * BLK : (i + 1) * BLK, :],
            slices_ref[i * BLK :, :],
            (((1,), (1,)), ((), ())),
            preferred_element_type=jnp.float32,
        )


def gram_kernel(count, slices_ref, packed_ref):
    packed_gram(slices_ref, packed_ref, count)


def rows_at(start, size):
    return pl.ds(pl.multiple_of(start, 8), size)


def pair_step(e, degree, source, older, target, st, potb, potx, shift=0, both_cells=True):
    at = lambda c, skip, size: pl.ds(pl.multiple_of(c * OWN + skip, 16), size)
    nodes = OWN + PLANE
    va, vb = source[at(e, 0, nodes), :], source[at(e + 1, 0, nodes), :]
    vp = source[at(e - 1, 0, nodes), :]
    both = jnp.dot(st[...], jnp.concatenate([va, vb], 1), preferred_element_type=jnp.float32)
    before = jnp.dot(st[OWN:nodes, :], vp, preferred_element_type=jnp.float32)
    scale = lambda c: potx[c][:, nodes:]
    wa, wb = va.astype(jnp.float32), vb.astype(jnp.float32)
    ya = scale(e) * both[:, :BLK] + potb[e] * wa
    yb = scale(e + 1) * both[:, BLK:] + potb[e + 1] * wb
    yp = scale(e - 1) * before + potb[e - 1, OWN:, :] * vp[OWN:].astype(jnp.float32)

    def finish(c, h, w, skip):
        size = h.shape[0]
        value = h - centre * w
        if degree == 1:
            value = value * (1.0 / half_width)
        else:
            value = value * (2.0 / half_width) - older[at(c, skip, size), :].astype(jnp.float32)
        target[at(c - shift, skip, size), :] = value.astype(target.dtype)

    if both_cells:
        finish(e, ya[:PLANE] + yp, wa[:PLANE], 0)
        finish(e, ya[PLANE:OWN], wa[PLANE:OWN], PLANE)
    finish(e + 1, yb[:PLANE] + ya[OWN:], wb[:PLANE], 0)
    finish(e + 1, yb[PLANE:OWN], wb[PLANE:OWN], PLANE)


def ahead_plan(bands):
    far = lambda i, j: bin(i ^ j).count("1") if bands == 4 else int(i != j)
    turns = {}
    plan = []
    for b in range(1, bands):
        for h in range(b):
            for q in [*range(b), *range(b + 1, bands)]:
                source = min((h, q), key=lambda i: (far(i, b), i != q))
                plan.append((far(source, b), source, b, h, q))
    ordered = []
    for _, source, b, h, q in sorted(plan):
        for part in range(2):
            turn = turns.get((source, b), 0)
            turns[source, b] = turn + 1
            ordered.append((turn, source, b, h, q, part))
    return sorted(ordered)


def part_start(part, each, bands):
    return part * each + jnp.where(part >= bands // 2, 2 * OWN, 0) if isinstance(part, jax.Array) else (
        part * each + (2 * OWN if part >= bands // 2 else 0)
    )


class Ahead:
    def __init__(self, bands, band, cell, slices, own, target, send_sem, recv_sem):
        self.band, self.bands = band, bands
        self.cell, self.slices, self.own, self.target = cell, slices, own, target
        self.send_sem, self.recv_sem = send_sem, recv_sem
        self.started, self.plan = [], ahead_plan(bands)
        self.count = [0] * bands

    def copy(self, slot, b, h, q, part, held):
        each = self.target.shape[2]
        size = each // 2
        n = q - (q > b)
        span = pl.ds(part * size, size)
        start = part_start(q, each, self.bands) + part * size
        source = self.slices.at[h, span] if held else self.own.at[pl.ds(start, size)]
        return pltpu.make_async_remote_copy(
            src_ref=source, dst_ref=self.target.at[h, n, span],
            send_sem=self.send_sem.at[slot],
            recv_sem=self.recv_sem.at[(h * (self.bands - 1) + n) * 2 + part],
            device_id={"band": b, "cell": self.cell}, device_id_type=MESH,
        )

    def start(self, first, last):
        for turn, source, b, h, q, part in self.plan:
            if first <= turn < last:
                slot = self.count[source]
                self.count[source] += 1
                copy = self.copy(slot, b, h, q, part, source == q)

                @pl.when(self.band == source)
                def _():
                    copy.start()

                self.started.append((source, b, copy))

    def finish(self):
        for source, b, copy in self.started:

            @pl.when(self.band == source)
            def _():
                copy.wait_send()

            @pl.when(self.band == b)
            def _():
                copy.wait_recv()


def filter_kernel(
    count, bands, cells, held, total,
    wave_ref, stiff_ref, scale_ref, potential_ref, slices_ref, three, ahead_ref, middle_ref, inverse_ref,
    pots, turned, ext, one, two, st, potx, potb,
    mine, from_core, half, from_band, quarter, from_z, piece, out_ref, work, parts,
    send_sem, recv_sem, ahead_send, ahead_recv, middle_send, middle_recv,
):
    band = lax.axis_index("band")
    cell = lax.axis_index("cell")
    core = lax.rem(cell, 2)
    level = lax.div(cell, 2)
    levels = cells // 2
    rows_half = mine.shape[0] // 2
    rows_band = rows_half // bands
    rows_z = rows_band // levels
    nodes = OWN + PLANE
    owned = held * OWN

    other_core = {"band": band, "cell": cell + 1 - 2 * core}
    band_peer = lambda o: lax.rem(band + o, bands)
    z_peer = lambda o: lax.rem(level + o, levels)
    band_device = lambda o: {"band": band_peer(o), "cell": cell}
    z_device = lambda o: {"band": band, "cell": z_peer(o) * 2 + core}
    cell_device = lambda o: {"band": band, "cell": lax.rem(cell + o, cells)}

    barrier = pltpu.get_barrier_semaphore()
    for o in range(1, bands):
        pl.semaphore_signal(barrier, inc=1, device_id=band_device(o), device_id_type=MESH)
    for o in range(1, cells):
        pl.semaphore_signal(barrier, inc=1, device_id=cell_device(o), device_id_type=MESH)
    used = [0]

    def send(src, dst, device):
        slot = used[0]
        used[0] += 1
        copy = pltpu.make_async_remote_copy(
            src_ref=src, dst_ref=dst, send_sem=send_sem.at[slot], recv_sem=recv_sem.at[slot],
            device_id=device, device_id_type=MESH,
        )
        copy.start()
        return copy

    low, high = 3 * OWN, 2 * OWN + PLANE
    right, left = cell_device(1), cell_device(cells - 1)

    def turn(q):
        span = slice(q * BLK, (q + 1) * BLK)
        turned[span, :] = wave_ref[:, span].T

    strips = owned // BLK
    first, last = -(-high // BLK), (owned - low) // BLK
    for c in range(held):
        pots[c, :, :nodes] = potential_ref[c : c + 1, :]
        pots[c, :, nodes:] = jnp.broadcast_to(scale_ref[:, c : c + 1], (1, BLK))
    for q in range(last, strips):
        turn(q)
    pl.semaphore_wait(barrier, bands - 1 + cells - 1)
    halo = [
        send(pots.at[held - 3 : held], potx.at[0:3], right),
        send(pots.at[0:2], potx.at[held + 3 : held + 5], left),
        send(turned.at[owned - low : owned], ext.at[0:low], right),
    ]
    for q in range(first):
        turn(q)
    halo.append(send(turned.at[0:high], ext.at[low + owned : low + owned + high], left))
    for q in range(first, last):
        turn(q)
    potx[3 : held + 3] = pots[...]
    ext[low : low + owned, :] = turned[...]
    st[...] = stiff_ref[...].T

    def columns(c):
        line = potx[c]
        for q in range(nodes // BLK):
            part = jnp.broadcast_to(line[:, q * BLK : (q + 1) * BLK], (BLK, BLK))
            potb[c, q * BLK : (q + 1) * BLK, :] = part.T

    @pl.loop(3, held + 3)
    def _(c):
        columns(c)

    mid, side = 2 + held // 2, held // 2 - 1
    each, quarter_each = ahead_ref.shape[2], slices_ref.shape[1] - ahead_ref.shape[2]
    middle = (mid - 3) * OWN

    @pl.loop(0, 3)
    def _(p):
        pair_step(mid - 2 + 2 * p, 1, ext, None, one, st, potb, potx)

    @pl.loop(0, 2)
    def _(p):
        pair_step(mid - 1 + 2 * p, 2, one, ext, two, st, potb, potx)

    pair_step(mid, 3, two, one, three, st, potb, potx, 3)

    def middle_copy(source, b, whole):
        start, size = (middle, 2 * OWN) if whole else (middle + b * quarter_each, quarter_each)
        target = middle_ref.at[source] if whole else slices_ref.at[source, pl.ds(each, quarter_each)]
        return pltpu.make_async_remote_copy(
            src_ref=three.at[pl.ds(start, size)], dst_ref=target,
            send_sem=middle_send.at[b], recv_sem=middle_recv.at[source],
            device_id={"band": b, "cell": cell}, device_id_type=MESH,
        )

    for b in reversed(range(bands)):
        for whole in (True, False):

            @pl.when(band < b if whole else band > b)
            def _():
                middle_copy(band, b, whole).start()

    for copy in halo:
        copy.wait()
    for c in (0, 1, 2, held + 3, held + 4):
        columns(c)
    outer = -(-(mid - 3) // 2)

    @pl.loop(0, 2 * outer)
    def _(p):
        e = jnp.where(p < outer, 1 + 2 * p, held + 3 - 2 * (p - outer))
        pair_step(e, 1, ext, None, one, st, potb, potx)

    @pl.loop(0, 2 * outer)
    def _(p):
        e = jnp.where(p < outer, 2 + 2 * p, held + 2 - 2 * (p - outer))
        pair_step(e, 2, one, ext, two, st, potb, potx)

    base = used[0]
    used[0] += bands - 1
    swaps = []
    near = lax.div(band, bands // 2)
    for upper in (1 - near, near):
        start = 3 + upper * (side + 2)

        @pl.loop(0, side // 2)
        def _(p):
            pair_step(start + 2 * p, 3, two, one, three, st, potb, potx, 3)

        if side % 2:
            pair_step(start + side - 2, 3, two, one, three, st, potb, potx, 3, both_cells=False)
        for n in range(bands // 2):
            part = upper * (bands // 2) + n
            from_row = part_start(part, each, bands)
            for o in range(1, bands):

                @pl.when(band_peer(o) == part)
                def _():
                    pltpu.make_async_remote_copy(
                        src_ref=three.at[pl.ds(pl.multiple_of(from_row, 16), each)],
                        dst_ref=slices_ref.at[band, pl.ds(0, each)],
                        send_sem=send_sem.at[base + o - 1], recv_sem=recv_sem.at[base + o - 1],
                        device_id=band_device(o), device_id_type=MESH,
                    ).start()

    own_row = pl.multiple_of(part_start(band, each, bands), 16)
    slices_ref[band, pl.ds(0, each), :] = three[pl.ds(own_row, each), :]
    own_row = pl.multiple_of(middle + band * quarter_each, 16)
    slices_ref[band, pl.ds(each, quarter_each), :] = three[pl.ds(own_row, quarter_each), :]
    for o in range(1, bands):
        swaps.append(
            pltpu.make_async_remote_copy(
                src_ref=three.at[pl.ds(0, each)], dst_ref=slices_ref.at[band, pl.ds(0, each)],
                send_sem=send_sem.at[base + o - 1], recv_sem=recv_sem.at[base + o - 1],
                device_id=band_device(o), device_id_type=MESH,
            )
        )
    for h in range(bands):
        for whole in (True, False):

            @pl.when(band > h if whole else band < h)
            def _():
                middle_copy(h, 0, whole).wait_recv()
                if whole:
                    row = pl.multiple_of(band * quarter_each, 16)
                    slices_ref[h, pl.ds(each, quarter_each), :] = middle_ref[h, pl.ds(row, quarter_each), :]

    for copy in swaps:
        copy.wait()
    ahead = Ahead(bands, band, cell, slices_ref, three, ahead_ref, ahead_send, ahead_recv)
    ahead.start(0, EARLY)

    for i in range(count):
        row, col = place(count - 1 - i, 0, count)
        width = (count - i) * BLK
        joined = jnp.concatenate([slices_ref[j] for j in range(i, count)], 1)
        mine[row : row + BLK, col : col + width] = jnp.dot(
            slices_ref[i].T, joined, preferred_element_type=jnp.float32
        )

    cuts = [0, (count + 2) // 2 * BLK, (count + 1) * BLK]
    spans = [slice(cuts[n], cuts[n + 1]) for n in range(2)]
    start_half = core * rows_half
    start_band = start_half + band * rows_band
    start_z = start_band + level * rows_z

    def each_span(stage):
        return [stage(span) for span in spans]

    def wait_all(copies):
        for copy in copies:
            copy.wait()

    over_core = each_span(
        lambda span: [
            send(
                mine.at[rows_at((1 - core) * rows_half, rows_half), span],
                from_core.at[:, span],
                other_core,
            )
        ]
    )
    over_band = []
    for span, copies in zip(spans, over_core):
        wait_all(copies)
        half[:, span] = mine[rows_at(start_half, rows_half), span] + from_core[:, span]
        over_band.append([
            send(
                half.at[rows_at(band_peer(o) * rows_band, rows_band), span],
                from_band.at[o - 1, :, span],
                band_device(o),
            )
            for o in range(1, bands)
        ])
    over_z = []
    for span, copies in zip(spans, over_band):
        wait_all(copies)
        summed = half[rows_at(band * rows_band, rows_band), span]
        for o in range(1, bands):
            summed = summed + from_band[o - 1, :, span]
        quarter[:, span] = summed
        over_z.append([
            send(
                quarter.at[rows_at(z_peer(o) * rows_z, rows_z), span],
                from_z.at[o - 1, :, span],
                z_device(o),
            )
            for o in range(1, levels)
        ])
    ahead.start(EARLY, EARLY + MIDDLE)
    back_z = []
    for span, copies in zip(spans, over_z):
        wait_all(copies)
        summed = quarter[rows_at(level * rows_z, rows_z), span]
        for o in range(1, levels):
            summed = summed + from_z[o - 1, :, span]
        summed = summed / total
        piece[:, span] = summed
        here = rows_at(start_z, rows_z)
        out_ref[here, span] = summed
        back_z.append([
            send(piece.at[:, span], out_ref.at[here, span], z_device(o)) for o in range(1, levels)
        ])
    back_band = []
    for span, copies in zip(spans, back_z):
        wait_all(copies)
        here = out_ref.at[rows_at(start_band, rows_band), span]
        back_band.append([send(here, here, band_device(o)) for o in range(1, bands)])
    back_core = []
    for span, copies in zip(spans, back_band):
        wait_all(copies)
        here = out_ref.at[rows_at(start_half, rows_half), span]
        back_core.append([send(here, here, other_core)])
    for copies in back_core:
        wait_all(copies)
    ahead.start(EARLY + MIDDLE, 1 << 10)
    factor_steps(count, out_ref, inverse_ref, work, parts)
    ahead.finish()
    for b in range(bands):
        for whole in (True, False):

            @pl.when(band < b if whole else band > b)
            def _():
                middle_copy(band, b, whole).wait_send()


def filtered(wavefunctions, stiffness, cell_scale, potential):
    bands, cells = lax.axis_size("band"), lax.axis_size("cell")
    band_rows, owned = wavefunctions.shape
    held = owned // OWN
    nodes = OWN + PLANE
    count = band_rows * bands // BLK
    quarter_each = 2 * OWN // bands
    each = owned // bands - quarter_each
    total = float(owned * cells)
    height, width = count * BLK // 2, (count + 1) * BLK
    levels = cells // 2
    rows_half = height // 2
    rows_band = rows_half // bands
    rows_z = rows_band // levels
    sends = 4 + (bands - 1) + 4 * (1 + (bands - 1) + (levels - 1))
    size = count * BLK
    plan = ahead_plan(bands)
    departs = max(sum(copy[1] == b for copy in plan) for b in range(bands))
    spans = owned + 5 * OWN + PLANE
    vmem = pl.BlockSpec(memory_space=pltpu.VMEM)
    f32, bf16 = jnp.float32, jnp.bfloat16
    return pl.pallas_call(
        functools.partial(filter_kernel, count, bands, cells, held, total),
        out_shape=(
            jax.ShapeDtypeStruct((bands, each + quarter_each, BLK), bf16),
            jax.ShapeDtypeStruct((owned, BLK), bf16),
            jax.ShapeDtypeStruct((bands - 1, bands - 1, each, BLK), bf16),
            jax.ShapeDtypeStruct((bands - 1, 2 * OWN, BLK), bf16),
            jax.ShapeDtypeStruct((size, size), bf16),
        ),
        in_specs=[vmem] * 4,
        out_specs=(vmem,) * 5,
        scratch_shapes=[
            pltpu.VMEM((held, 1, nodes + BLK), f32),
            pltpu.VMEM((owned, BLK), bf16),
            pltpu.VMEM((spans, BLK), bf16),
            pltpu.VMEM((spans, BLK), bf16),
            pltpu.VMEM((spans, BLK), bf16),
            pltpu.VMEM((nodes, nodes), bf16),
            pltpu.VMEM((held + 5, 1, nodes + BLK), f32),
            pltpu.VMEM((held + 5, nodes, BLK), f32),
            pltpu.VMEM((height, width), f32),
            pltpu.VMEM((rows_half, width), f32),
            pltpu.VMEM((rows_half, width), f32),
            pltpu.VMEM((bands - 1, rows_band, width), f32),
            pltpu.VMEM((rows_band, width), f32),
            pltpu.VMEM((levels - 1, rows_z, width), f32),
            pltpu.VMEM((rows_z, width), f32),
            pltpu.VMEM((height, width), f32),
            pltpu.VMEM((size, size), f32),
            pltpu.VMEM((2, 3 * SUB, size), bf16),
            pltpu.SemaphoreType.DMA((sends,)),
            pltpu.SemaphoreType.DMA((sends,)),
            pltpu.SemaphoreType.DMA((departs,)),
            pltpu.SemaphoreType.DMA((2 * (bands - 1) ** 2,)),
            pltpu.SemaphoreType.DMA((bands,)),
            pltpu.SemaphoreType.DMA((bands,)),
        ],
        compiler_params=pltpu.CompilerParams(collective_id=0, has_side_effects=True),
    )(wavefunctions, stiffness, cell_scale[None, :], potential)


def rotate_kernel(bands, inverse_ref, slices_ref, own_ref, ahead_ref, middle_ref, out_ref):
    band = lax.axis_index("band")
    each = ahead_ref.shape[2]
    middle = bands // 2 * each
    edges = [(part_start(q, each, bands), q) for q in range(bands)] + [(middle, None)]

    def rows(g, h, first, last):
        found = []
        for start, q in sorted(edges, key=lambda edge: edge[0]):
            low, high = max(first, start), min(last, start + (2 * OWN if q is None else each))
            if low < high:
                span = slice(low - start, high - start)
                found.append(
                    middle_ref[h, span] if q is None else slices_ref[h, span] if q == g
                    else ahead_ref[h, q - (q > g), span]
                )
        return jnp.concatenate(found, 0)

    for g in range(bands):

        @pl.when(band == g)
        def _():
            some = inverse_ref[g * BLK : (g + 1) * BLK, : (g + 1) * BLK]
            for first in range(0, own_ref.shape[0], 2 * OWN):
                here = slice(first, first + 2 * OWN)
                joined = [rows(g, h, here.start, here.stop) for h in range(g)] + [own_ref[here, :]]
                out_ref[:, here] = lax.dot_general(
                    some, jnp.concatenate(joined, 1), (((1,), (1,)), ((), ())),
                    preferred_element_type=jnp.float32,
                ).astype(out_ref.dtype)


def rotated_here(inverse, slices, own, ahead, middle):
    bands = slices.shape[0]
    vmem = pl.BlockSpec(memory_space=pltpu.VMEM)
    return pl.pallas_call(
        functools.partial(rotate_kernel, bands),
        out_shape=jax.ShapeDtypeStruct(own.shape[::-1], own.dtype),
        in_specs=[vmem] * 5,
        out_specs=vmem,
    )(inverse, slices, own, ahead, middle)


def fits(band_rows, owned, bands, cells):
    height = band_rows * bands // 2
    return (
        band_rows == BLK
        and owned % OWN == 0
        and bands >= 3
        and bands % 2 == 0
        and cells % 2 == 0
        and cells >= 4
        and owned // OWN >= 8
        and owned // OWN % 2 == 0
        and 2 * OWN % (16 * bands) == 0
        and (owned - 2 * OWN) % (32 * bands) == 0
        and height % (16 * bands * (cells // 2)) == 0
    )


def margin_packed(slices):
    bands, cells = lax.axis_size("band"), lax.axis_size("cell")
    band_total, nodes = slices.shape
    count = band_total // BLK
    shape = jax.ShapeDtypeStruct((band_total // 2, (count + 1) * BLK), jnp.float32)
    vmem = pl.BlockSpec(memory_space=pltpu.VMEM)
    partial = pl.pallas_call(
        functools.partial(gram_kernel, count), out_shape=shape, in_specs=[vmem], out_specs=vmem
    )(slices)
    return lax.psum(partial, ("band", "cell")) / float(nodes * bands * cells)


def eliminate(work, k, later):
    groups, tiles = work.shape[1] // BLK, SUB // PAN
    home, offset = k // BLK, k % BLK
    shape = (PAN, BLK)
    lane = lax.broadcasted_iota(jnp.int32, shape, 1)
    row = lax.broadcasted_iota(jnp.int32, shape, 0)
    part = lambda t, q: (slice(k + t * PAN, k + (t + 1) * PAN), slice(q * BLK, (q + 1) * BLK))
    left = [work[part(t, home)] for t in range(tiles)]
    inside = (lane >= offset) & (lane < offset + SUB)
    right = []
    for t in range(tiles):
        unit = jnp.where(lane == row + (offset + t * PAN), 1.0, 0.0)
        right.append(
            [jnp.where(inside, unit, left[t]) if q == home else work[part(t, q)] for q in range(groups)]
        )
    spread = lambda value: jnp.broadcast_to(value, shape)
    lanes = lambda value, c: jnp.take_along_axis(value, jnp.full(shape, c, jnp.int32), axis=1)
    for m in range(tiles):
        c, more = offset + m * PAN, m + 1 < tiles
        here = range(m, tiles)
        cols = {t: [lanes(left[t], c + j) for j in range(PAN)] for t in here}
        grid = [[spread(cols[m][j][i : i + 1, :]) for i in range(j, PAN)] for j in range(PAN)]
        for j in range(PAN):
            scale = lax.rsqrt(grid[j][0])
            factor = {i: grid[j][i - j] * scale for i in range(j + 1, PAN)}
            for q in range(j + 1, PAN):
                grid[q] = [grid[q][i - q] - factor[i] * factor[q] for i in range(q, PAN)]
            head = {t: cols[t][j] * scale for t in here}
            below = jnp.where(row > j, head[m], 0.0)
            pivot = [spread(value[j : j + 1, :]) * scale for value in right[m]]
            right[m] = [
                jnp.where(row == j, p, value - below * p) for p, value in zip(pivot, right[m])
            ]
            if more:
                ahead = spread(left[m][j : j + 1, :]) * scale
                left[m] = left[m] - below * ahead
            for t in here[1:]:
                right[t] = [value - head[t] * p for p, value in zip(pivot, right[t])]
                left[t] = left[t] - head[t] * ahead
            for i in range(j + 1, PAN):
                for t in here:
                    cols[t][i] = cols[t][i] - factor[i] * head[t]
        for q in range(groups):
            work[part(m, q)] = right[m][q]
        for task in later[m::tiles]:
            task()


def split_rows(work, parts, k):
    rest = work[k : k + SUB, :]
    for n in range(3):
        term = rest.astype(jnp.bfloat16)
        parts[n * SUB : (n + 1) * SUB, :] = term
        rest = rest - term.astype(jnp.float32)


def update_below(work, parts, k, first, last):
    size = work.shape[1]
    home, h = k // BLK, first // BLK
    rows, block = slice(first, last), slice(h * BLK, (h + 1) * BLK)
    term = lambda n, span: parts[n * SUB : (n + 1) * SUB, span]
    turned = jnp.concatenate([term(n, block) for n in (0, 1, 2, 0)], 0).T
    turned = turned[first - h * BLK : last - h * BLK]
    mult = jnp.concatenate([turned, turned], 1)
    for low, high in ((0, home + 1), (max(h, home + 1), size // BLK)):
        if low < high:
            span = slice(low * BLK, high * BLK)
            old = work[rows, span]
            if low <= home < high:
                lane = lax.broadcasted_iota(jnp.int32, old.shape, 1) + low * BLK
                old = jnp.where((lane >= k) & (lane < k + SUB), 0.0, old)
            none = jnp.zeros((2 * SUB, (high - low) * BLK), jnp.bfloat16)
            terms = [term(n, span) for n in (0, 0, 0, 1, 2, 1)] + [none]
            work[rows, span] = old - jnp.dot(
                mult, jnp.concatenate(terms, 0), preferred_element_type=jnp.float32
            )


def factor_steps(count, packed_ref, out_ref, work, parts):
    size = count * BLK
    for i in range(count):
        row, col = place(count - 1 - i, 0, count)
        width = (count - i) * BLK
        work[i * BLK : (i + 1) * BLK, i * BLK :] = packed_ref[row : row + BLK, col : col + width]
    later = []
    for k in range(0, size, SUB):
        eliminate(work, k, later)
        half = parts.at[k // SUB % 2]
        if k + SUB < size:
            split_rows(work, half, k)
            update_below(work, half, k, k + SUB, k + 2 * SUB)
        starts = [k + 2 * SUB, *range((k + 2 * SUB) // BLK * BLK + BLK, size, BLK)]
        later = [
            functools.partial(update_below, work, half, k, first, first // BLK * BLK + BLK)
            for first in starts
            if first < size
        ]
    for k in range(0, size, SUB):
        lane = lax.broadcasted_iota(jnp.int32, (SUB, size), 1)
        kept = jnp.where(lane < k + SUB, work[k : k + SUB, :], 0.0)
        out_ref[k : k + SUB, :] = kept.astype(out_ref.dtype)


def inverse_factor(packed):
    size = packed.shape[0] * 2
    count = size // BLK
    vmem = pl.BlockSpec(memory_space=pltpu.VMEM)
    return pl.pallas_call(
        functools.partial(factor_steps, count),
        out_shape=jax.ShapeDtypeStruct((size, size), jnp.bfloat16),
        in_specs=[vmem],
        out_specs=vmem,
        scratch_shapes=[
            pltpu.VMEM((size, size), jnp.float32),
            pltpu.VMEM((2, 3 * SUB, size), jnp.bfloat16),
        ],
    )(packed)


def shards(wavefunctions, stiffness, cell_scale, potential):
    if fits(*wavefunctions.shape, lax.axis_size("band"), lax.axis_size("cell")):
        slices, own, ahead, middle, inverse = filtered(
            wavefunctions, stiffness, cell_scale, potential
        )
        return rotated_here(inverse, slices, own, ahead, middle)
    anchor = wavefunctions.astype(jnp.float32)
    degree_one = (
        (apply_h(wavefunctions, stiffness, cell_scale, potential) - centre * anchor) / half_width
    ).astype(jnp.bfloat16)
    one_wide = degree_one.astype(jnp.float32)
    degree_two = (
        2.0
        * (apply_h(degree_one, stiffness, cell_scale, potential) - centre * one_wide)
        / half_width
        - anchor
    ).astype(jnp.bfloat16)
    two_wide = degree_two.astype(jnp.float32)
    degree_three = (
        2.0
        * (apply_h(degree_two, stiffness, cell_scale, potential) - centre * two_wide)
        / half_width
        - one_wide
    ).astype(jnp.bfloat16)
    slices = lax.all_to_all(degree_three, "band", split_axis=1, concat_axis=0, tiled=True)
    inverse = inverse_factor(margin_packed(slices))
    rotated = jnp.dot(inverse, slices, preferred_element_type=jnp.float32).astype(jnp.bfloat16)
    return lax.all_to_all(rotated, "band", split_axis=0, concat_axis=1, tiled=True)


def solution(mesh):
    in_specs = (P("band", "cell"), P(), P("cell"), P("cell", None))
    out_specs = P("band", "cell")
    return jax.shard_map(shards, mesh=mesh, in_specs=in_specs, out_specs=out_specs, check_vma=False)
```

```python
import functools
import jax
import jax.numpy as jnp
from jax import lax
from jax.experimental import pallas as pl
from jax.experimental.pallas import tpu as pltpu
from jax.sharding import PartitionSpec as P

PLANE = 64
OWN = 448
BLK = 128
PAN = 8
SUB = 32
EARLY = 1
MIDDLE = 3
MESH = pl.DeviceIdType.MESH

centre = 4.0
half_width = 3.0


def shifted(block, axis, distance):
    devices = range(lax.axis_size(axis))
    route = [((i - distance) % len(devices), i) for i in devices]
    return lax.ppermute(block, axis, route)


def apply_h(field, stiffness, cell_scale, potential):
    band_rows = field.shape[0]
    cell_count = field.shape[1] // OWN
    following = shifted(field[:, :PLANE], "cell", -1)
    owned_part = field.reshape(band_rows, cell_count, OWN)
    top_plane = jnp.concatenate([owned_part[:, 1:, :PLANE], following[:, None, :]], 1)
    cell_nodes = jnp.concatenate([owned_part, top_plane], 2)
    stiff_part = jnp.einsum(
        "bcn,nm->bcm", cell_nodes, stiffness, preferred_element_type=jnp.float32
    )
    cell_result = cell_scale[None, :, None] * stiff_part + potential[None] * cell_nodes.astype(
        jnp.float32
    )
    spill = cell_result[:, :, OWN:]
    incoming = shifted(spill[:, -1], "cell", 1)
    spill = jnp.concatenate([incoming[:, None, :], spill[:, :-1]], 1)
    kept = cell_result[:, :, :OWN]
    kept = jnp.concatenate([kept[:, :, :PLANE] + spill, kept[:, :, PLANE:]], 2)
    return kept.reshape(band_rows, cell_count * OWN)


def place(i, j, count):
    tall = count // 2
    n = j if i == 0 else count + (j - i) + sum(count - m for m in range(1, i))
    return slice(n % tall * BLK, (n % tall + 1) * BLK), slice(n // tall * BLK, (n // tall + 1) * BLK)


def pack(packed_ref, row_of_blocks, i, count):
    for j in range(i, count):
        packed_ref[place(i, j, count)] = row_of_blocks[:, (j - i) * BLK : (j - i + 1) * BLK]


def packed_gram(slices_ref, packed_ref, count):
    for i in range(count):
        product = lax.dot_general(
            slices_ref[i * BLK : (i + 1) * BLK, :],
            slices_ref[i * BLK :, :],
            (((1,), (1,)), ((), ())),
            preferred_element_type=jnp.float32,
        )
        pack(packed_ref, product, i, count)


def gram_kernel(count, slices_ref, packed_ref):
    packed_gram(slices_ref, packed_ref, count)


def rows_at(start, size):
    return pl.ds(pl.multiple_of(start, 8), size)


def pair_step(e, degree, source, older, target, st, potb, potx, shift=0, both_cells=True):
    at = lambda c, skip, size: pl.ds(pl.multiple_of(c * OWN + skip, 16), size)
    nodes = OWN + PLANE
    va, vb = source[at(e, 0, nodes), :], source[at(e + 1, 0, nodes), :]
    vp = source[at(e - 1, 0, nodes), :]
    both = jnp.dot(st[...], jnp.concatenate([va, vb], 1), preferred_element_type=jnp.float32)
    before = jnp.dot(st[OWN:nodes, :], vp, preferred_element_type=jnp.float32)
    scale = lambda c: potx[c][:, nodes:]
    wa, wb = va.astype(jnp.float32), vb.astype(jnp.float32)
    ya = scale(e) * both[:, :BLK] + potb[e] * wa
    yb = scale(e + 1) * both[:, BLK:] + potb[e + 1] * wb
    yp = scale(e - 1) * before + potb[e - 1, OWN:, :] * vp[OWN:].astype(jnp.float32)

    def finish(c, h, w, skip):
        size = h.shape[0]
        value = h - centre * w
        if degree == 1:
            value = value * (1.0 / half_width)
        else:
            value = value * (2.0 / half_width) - older[at(c, skip, size), :].astype(jnp.float32)
        target[at(c - shift, skip, size), :] = value.astype(target.dtype)

    if both_cells:
        finish(e, ya[:PLANE] + yp, wa[:PLANE], 0)
        finish(e, ya[PLANE:OWN], wa[PLANE:OWN], PLANE)
    finish(e + 1, yb[:PLANE] + ya[OWN:], wb[:PLANE], 0)
    finish(e + 1, yb[PLANE:OWN], wb[PLANE:OWN], PLANE)


def ahead_plan(bands):
    far = lambda i, j: bin(i ^ j).count("1") if bands == 4 else int(i != j)
    turns = {}
    plan = []
    for b in range(1, bands):
        for h in range(b):
            for q in [*range(b), *range(b + 1, bands)]:
                source = min((h, q), key=lambda i: (far(i, b), i != q))
                plan.append((far(source, b), source, b, h, q))
    ordered = []
    for _, source, b, h, q in sorted(plan):
        for part in range(2):
            turn = turns.get((source, b), 0)
            turns[source, b] = turn + 1
            ordered.append((turn, source, b, h, q, part))
    return sorted(ordered)


def part_start(part, each, bands):
    return part * each + jnp.where(part >= bands // 2, 2 * OWN, 0) if isinstance(part, jax.Array) else (
        part * each + (2 * OWN if part >= bands // 2 else 0)
    )


class Ahead:
    def __init__(self, bands, band, cell, slices, own, target, send_sem, recv_sem):
        self.band, self.bands = band, bands
        self.cell, self.slices, self.own, self.target = cell, slices, own, target
        self.send_sem, self.recv_sem = send_sem, recv_sem
        self.started, self.plan = [], ahead_plan(bands)
        self.count = [0] * bands

    def copy(self, slot, b, h, q, part, held):
        each = self.target.shape[2]
        size = each // 2
        n = q - (q > b)
        span = pl.ds(part * size, size)
        start = part_start(q, each, self.bands) + part * size
        source = self.slices.at[h, span] if held else self.own.at[pl.ds(start, size)]
        return pltpu.make_async_remote_copy(
            src_ref=source, dst_ref=self.target.at[h, n, span],
            send_sem=self.send_sem.at[slot],
            recv_sem=self.recv_sem.at[(h * (self.bands - 1) + n) * 2 + part],
            device_id={"band": b, "cell": self.cell}, device_id_type=MESH,
        )

    def start(self, first, last):
        for turn, source, b, h, q, part in self.plan:
            if first <= turn < last:
                slot = self.count[source]
                self.count[source] += 1
                copy = self.copy(slot, b, h, q, part, source == q)

                @pl.when(self.band == source)
                def _():
                    copy.start()

                self.started.append((source, b, copy))

    def finish(self):
        for source, b, copy in self.started:

            @pl.when(self.band == source)
            def _():
                copy.wait_send()

            @pl.when(self.band == b)
            def _():
                copy.wait_recv()


def filter_kernel(
    count, bands, cells, held, total,
    wave_ref, stiff_ref, scale_ref, potential_ref, slices_ref, three, ahead_ref, middle_ref, inverse_ref,
    pots, turned, ext, one, two, st, potx, potb,
    mine, from_core, half, from_band, quarter, from_z, piece, out_ref, work, parts, lower,
    send_sem, recv_sem, ahead_send, ahead_recv, middle_send, middle_recv,
):
    band = lax.axis_index("band")
    cell = lax.axis_index("cell")
    core = lax.rem(cell, 2)
    level = lax.div(cell, 2)
    levels = cells // 2
    rows_half = mine.shape[0] // 2
    rows_band = rows_half // bands
    rows_z = rows_band // levels
    nodes = OWN + PLANE
    owned = held * OWN

    other_core = {"band": band, "cell": cell + 1 - 2 * core}
    band_peer = lambda o: lax.rem(band + o, bands)
    z_peer = lambda o: lax.rem(level + o, levels)
    band_device = lambda o: {"band": band_peer(o), "cell": cell}
    z_device = lambda o: {"band": band, "cell": z_peer(o) * 2 + core}
    cell_device = lambda o: {"band": band, "cell": lax.rem(cell + o, cells)}

    barrier = pltpu.get_barrier_semaphore()
    for o in range(1, bands):
        pl.semaphore_signal(barrier, inc=1, device_id=band_device(o), device_id_type=MESH)
    for o in range(1, cells):
        pl.semaphore_signal(barrier, inc=1, device_id=cell_device(o), device_id_type=MESH)
    used = [0]

    def send(src, dst, device):
        slot = used[0]
        used[0] += 1
        copy = pltpu.make_async_remote_copy(
            src_ref=src, dst_ref=dst, send_sem=send_sem.at[slot], recv_sem=recv_sem.at[slot],
            device_id=device, device_id_type=MESH,
        )
        copy.start()
        return copy

    low, high = 3 * OWN, 2 * OWN + PLANE
    right, left = cell_device(1), cell_device(cells - 1)

    def turn(q):
        span = slice(q * BLK, (q + 1) * BLK)
        turned[span, :] = wave_ref[:, span].T

    strips = owned // BLK
    first, last = -(-high // BLK), (owned - low) // BLK
    for c in range(held):
        pots[c, :, :nodes] = potential_ref[c : c + 1, :]
        pots[c, :, nodes:] = jnp.broadcast_to(scale_ref[:, c : c + 1], (1, BLK))
    for q in range(last, strips):
        turn(q)
    pl.semaphore_wait(barrier, bands - 1 + cells - 1)
    halo = [
        send(pots.at[held - 3 : held], potx.at[0:3], right),
        send(pots.at[0:2], potx.at[held + 3 : held + 5], left),
        send(turned.at[owned - low : owned], ext.at[0:low], right),
    ]
    for q in range(first):
        turn(q)
    halo.append(send(turned.at[0:high], ext.at[low + owned : low + owned + high], left))
    for q in range(first, last):
        turn(q)
    potx[3 : held + 3] = pots[...]
    ext[low : low + owned, :] = turned[...]
    st[...] = stiff_ref[...].T

    def columns(c):
        line = potx[c]
        for q in range(nodes // BLK):
            part = jnp.broadcast_to(line[:, q * BLK : (q + 1) * BLK], (BLK, BLK))
            potb[c, q * BLK : (q + 1) * BLK, :] = part.T

    @pl.loop(3, held + 3)
    def _(c):
        columns(c)

    mid, side = 2 + held // 2, held // 2 - 1
    each, quarter_each = ahead_ref.shape[2], slices_ref.shape[1] - ahead_ref.shape[2]
    middle = (mid - 3) * OWN

    @pl.loop(0, 3)
    def _(p):
        pair_step(mid - 2 + 2 * p, 1, ext, None, one, st, potb, potx)

    @pl.loop(0, 2)
    def _(p):
        pair_step(mid - 1 + 2 * p, 2, one, ext, two, st, potb, potx)

    pair_step(mid, 3, two, one, three, st, potb, potx, 3)

    def middle_copy(source, b, whole):
        start, size = (middle, 2 * OWN) if whole else (middle + b * quarter_each, quarter_each)
        target = middle_ref.at[source] if whole else slices_ref.at[source, pl.ds(each, quarter_each)]
        return pltpu.make_async_remote_copy(
            src_ref=three.at[pl.ds(start, size)], dst_ref=target,
            send_sem=middle_send.at[b], recv_sem=middle_recv.at[source],
            device_id={"band": b, "cell": cell}, device_id_type=MESH,
        )

    for b in reversed(range(bands)):
        for whole in (True, False):

            @pl.when(band < b if whole else band > b)
            def _():
                middle_copy(band, b, whole).start()

    for copy in halo:
        copy.wait()
    for c in (0, 1, 2, held + 3, held + 4):
        columns(c)
    outer = -(-(mid - 3) // 2)

    @pl.loop(0, 2 * outer)
    def _(p):
        e = jnp.where(p < outer, 1 + 2 * p, held + 3 - 2 * (p - outer))
        pair_step(e, 1, ext, None, one, st, potb, potx)

    @pl.loop(0, 2 * outer)
    def _(p):
        e = jnp.where(p < outer, 2 + 2 * p, held + 2 - 2 * (p - outer))
        pair_step(e, 2, one, ext, two, st, potb, potx)

    base = used[0]
    used[0] += bands - 1
    swaps = []
    near = lax.div(band, bands // 2)
    for upper in (1 - near, near):
        start = 3 + upper * (side + 2)

        @pl.loop(0, side // 2)
        def _(p):
            pair_step(start + 2 * p, 3, two, one, three, st, potb, potx, 3)

        if side % 2:
            pair_step(start + side - 2, 3, two, one, three, st, potb, potx, 3, both_cells=False)
        for n in range(bands // 2):
            part = upper * (bands // 2) + n
            from_row = part_start(part, each, bands)
            for o in range(1, bands):

                @pl.when(band_peer(o) == part)
                def _():
                    pltpu.make_async_remote_copy(
                        src_ref=three.at[pl.ds(pl.multiple_of(from_row, 16), each)],
                        dst_ref=slices_ref.at[band, pl.ds(0, each)],
                        send_sem=send_sem.at[base + o - 1], recv_sem=recv_sem.at[base + o - 1],
                        device_id=band_device(o), device_id_type=MESH,
                    ).start()

    own_row = pl.multiple_of(part_start(band, each, bands), 16)
    slices_ref[band, pl.ds(0, each), :] = three[pl.ds(own_row, each), :]
    own_row = pl.multiple_of(middle + band * quarter_each, 16)
    slices_ref[band, pl.ds(each, quarter_each), :] = three[pl.ds(own_row, quarter_each), :]
    for o in range(1, bands):
        swaps.append(
            pltpu.make_async_remote_copy(
                src_ref=three.at[pl.ds(0, each)], dst_ref=slices_ref.at[band, pl.ds(0, each)],
                send_sem=send_sem.at[base + o - 1], recv_sem=recv_sem.at[base + o - 1],
                device_id=band_device(o), device_id_type=MESH,
            )
        )
    for h in range(bands):
        for whole in (True, False):

            @pl.when(band > h if whole else band < h)
            def _():
                middle_copy(h, 0, whole).wait_recv()
                if whole:
                    row = pl.multiple_of(band * quarter_each, 16)
                    slices_ref[h, pl.ds(each, quarter_each), :] = middle_ref[h, pl.ds(row, quarter_each), :]

    for copy in swaps:
        copy.wait()
    ahead = Ahead(bands, band, cell, slices_ref, three, ahead_ref, ahead_send, ahead_recv)
    ahead.start(0, EARLY)

    for i in range(count):
        joined = jnp.concatenate([slices_ref[j] for j in range(i, count)], 1)
        product = jnp.dot(slices_ref[i].T, joined, preferred_element_type=jnp.float32)
        pack(mine, product, i, count)

    cuts = [0, 2 * BLK, (count + 1) * BLK]
    spans = [slice(cuts[n], cuts[n + 1]) for n in range(2)]
    start_half = core * rows_half
    start_band = start_half + band * rows_band
    start_z = start_band + level * rows_z

    def each_span(stage):
        return [stage(span) for span in spans]

    def wait_all(copies):
        for copy in copies:
            copy.wait()

    over_core = each_span(
        lambda span: [
            send(
                mine.at[rows_at((1 - core) * rows_half, rows_half), span],
                from_core.at[:, span],
                other_core,
            )
        ]
    )
    over_band = []
    for span, copies in zip(spans, over_core):
        wait_all(copies)
        half[:, span] = mine[rows_at(start_half, rows_half), span] + from_core[:, span]
        over_band.append([
            send(
                half.at[rows_at(band_peer(o) * rows_band, rows_band), span],
                from_band.at[o - 1, :, span],
                band_device(o),
            )
            for o in range(1, bands)
        ])
    over_z = []
    for span, copies in zip(spans, over_band):
        wait_all(copies)
        summed = half[rows_at(band * rows_band, rows_band), span]
        for o in range(1, bands):
            summed = summed + from_band[o - 1, :, span]
        quarter[:, span] = summed
        over_z.append([
            send(
                quarter.at[rows_at(z_peer(o) * rows_z, rows_z), span],
                from_z.at[o - 1, :, span],
                z_device(o),
            )
            for o in range(1, levels)
        ])
    ahead.start(EARLY, EARLY + MIDDLE)
    back_z = []
    for span, copies in zip(spans, over_z):
        wait_all(copies)
        summed = quarter[rows_at(level * rows_z, rows_z), span]
        for o in range(1, levels):
            summed = summed + from_z[o - 1, :, span]
        summed = summed / total
        piece[:, span] = summed
        here = rows_at(start_z, rows_z)
        out_ref[here, span] = summed
        back_z.append([
            send(piece.at[:, span], out_ref.at[here, span], z_device(o)) for o in range(1, levels)
        ])
    back_band = []
    for span, copies in zip(spans, back_z):
        wait_all(copies)
        here = out_ref.at[rows_at(start_band, rows_band), span]
        back_band.append([send(here, here, band_device(o)) for o in range(1, bands)])
    def to_core(n):
        wait_all(back_band[n])
        here = out_ref.at[rows_at(start_half, rows_half), spans[n]]
        return send(here, here, other_core)

    def rest_to_core():
        back_core.append(to_core(1))
        ahead.start(EARLY + MIDDLE, 1 << 10)

    back_core = [to_core(0)]
    back_core[0].wait()
    factor_steps(
        count, out_ref, inverse_ref, work, parts, lower, rest_to_core, lambda: back_core[1].wait()
    )
    ahead.finish()
    for b in range(bands):
        for whole in (True, False):

            @pl.when(band < b if whole else band > b)
            def _():
                middle_copy(band, b, whole).wait_send()


def filtered(wavefunctions, stiffness, cell_scale, potential):
    bands, cells = lax.axis_size("band"), lax.axis_size("cell")
    band_rows, owned = wavefunctions.shape
    held = owned // OWN
    nodes = OWN + PLANE
    count = band_rows * bands // BLK
    quarter_each = 2 * OWN // bands
    each = owned // bands - quarter_each
    total = float(owned * cells)
    height, width = count * BLK // 2, (count + 1) * BLK
    levels = cells // 2
    rows_half = height // 2
    rows_band = rows_half // bands
    rows_z = rows_band // levels
    sends = 4 + (bands - 1) + 4 * (1 + (bands - 1) + (levels - 1))
    size = count * BLK
    plan = ahead_plan(bands)
    departs = max(sum(copy[1] == b for copy in plan) for b in range(bands))
    spans = owned + 5 * OWN + PLANE
    vmem = pl.BlockSpec(memory_space=pltpu.VMEM)
    f32, bf16 = jnp.float32, jnp.bfloat16
    return pl.pallas_call(
        functools.partial(filter_kernel, count, bands, cells, held, total),
        out_shape=(
            jax.ShapeDtypeStruct((bands, each + quarter_each, BLK), bf16),
            jax.ShapeDtypeStruct((owned, BLK), bf16),
            jax.ShapeDtypeStruct((bands - 1, bands - 1, each, BLK), bf16),
            jax.ShapeDtypeStruct((bands - 1, 2 * OWN, BLK), bf16),
            jax.ShapeDtypeStruct((size, size), bf16),
        ),
        in_specs=[vmem] * 4,
        out_specs=(vmem,) * 5,
        scratch_shapes=[
            pltpu.VMEM((held, 1, nodes + BLK), f32),
            pltpu.VMEM((owned, BLK), bf16),
            pltpu.VMEM((spans, BLK), bf16),
            pltpu.VMEM((spans, BLK), bf16),
            pltpu.VMEM((spans, BLK), bf16),
            pltpu.VMEM((nodes, nodes), bf16),
            pltpu.VMEM((held + 5, 1, nodes + BLK), f32),
            pltpu.VMEM((held + 5, nodes, BLK), f32),
            pltpu.VMEM((height, width), f32),
            pltpu.VMEM((rows_half, width), f32),
            pltpu.VMEM((rows_half, width), f32),
            pltpu.VMEM((bands - 1, rows_band, width), f32),
            pltpu.VMEM((rows_band, width), f32),
            pltpu.VMEM((levels - 1, rows_z, width), f32),
            pltpu.VMEM((rows_z, width), f32),
            pltpu.VMEM((height, width), f32),
            pltpu.VMEM((size, size), f32),
            pltpu.VMEM((size // SUB, 3 * SUB, size), bf16),
            pltpu.VMEM((BLK // SUB, 3 * SUB, BLK), bf16),
            pltpu.SemaphoreType.DMA((sends,)),
            pltpu.SemaphoreType.DMA((sends,)),
            pltpu.SemaphoreType.DMA((departs,)),
            pltpu.SemaphoreType.DMA((2 * (bands - 1) ** 2,)),
            pltpu.SemaphoreType.DMA((bands,)),
            pltpu.SemaphoreType.DMA((bands,)),
        ],
        compiler_params=pltpu.CompilerParams(collective_id=0, has_side_effects=True),
    )(wavefunctions, stiffness, cell_scale[None, :], potential)


def rotate_kernel(bands, inverse_ref, slices_ref, own_ref, ahead_ref, middle_ref, out_ref):
    band = lax.axis_index("band")
    each = ahead_ref.shape[2]
    middle = bands // 2 * each
    edges = [(part_start(q, each, bands), q) for q in range(bands)] + [(middle, None)]

    def rows(g, h, first, last):
        found = []
        for start, q in sorted(edges, key=lambda edge: edge[0]):
            low, high = max(first, start), min(last, start + (2 * OWN if q is None else each))
            if low < high:
                span = slice(low - start, high - start)
                found.append(
                    middle_ref[h, span] if q is None else slices_ref[h, span] if q == g
                    else ahead_ref[h, q - (q > g), span]
                )
        return jnp.concatenate(found, 0)

    for g in range(bands):

        @pl.when(band == g)
        def _():
            some = inverse_ref[g * BLK : (g + 1) * BLK, : (g + 1) * BLK]
            for first in range(0, own_ref.shape[0], 2 * OWN):
                here = slice(first, first + 2 * OWN)
                joined = [rows(g, h, here.start, here.stop) for h in range(g)] + [own_ref[here, :]]
                out_ref[:, here] = lax.dot_general(
                    some, jnp.concatenate(joined, 1), (((1,), (1,)), ((), ())),
                    preferred_element_type=jnp.float32,
                ).astype(out_ref.dtype)


def rotated_here(inverse, slices, own, ahead, middle):
    bands = slices.shape[0]
    vmem = pl.BlockSpec(memory_space=pltpu.VMEM)
    return pl.pallas_call(
        functools.partial(rotate_kernel, bands),
        out_shape=jax.ShapeDtypeStruct(own.shape[::-1], own.dtype),
        in_specs=[vmem] * 5,
        out_specs=vmem,
    )(inverse, slices, own, ahead, middle)


def fits(band_rows, owned, bands, cells):
    height = band_rows * bands // 2
    return (
        band_rows == BLK
        and owned % OWN == 0
        and bands >= 3
        and bands % 2 == 0
        and cells % 2 == 0
        and cells >= 4
        and owned // OWN >= 8
        and owned // OWN % 2 == 0
        and 2 * OWN % (16 * bands) == 0
        and (owned - 2 * OWN) % (32 * bands) == 0
        and height % (16 * bands * (cells // 2)) == 0
    )


def margin_packed(slices):
    bands, cells = lax.axis_size("band"), lax.axis_size("cell")
    band_total, nodes = slices.shape
    count = band_total // BLK
    shape = jax.ShapeDtypeStruct((band_total // 2, (count + 1) * BLK), jnp.float32)
    vmem = pl.BlockSpec(memory_space=pltpu.VMEM)
    partial = pl.pallas_call(
        functools.partial(gram_kernel, count), out_shape=shape, in_specs=[vmem], out_specs=vmem
    )(slices)
    return lax.psum(partial, ("band", "cell")) / float(nodes * bands * cells)


def eliminate(work, k, later):
    groups, tiles = work.shape[1] // BLK, SUB // PAN
    home, offset = k // BLK, k % BLK
    shape = (PAN, BLK)
    lane = lax.broadcasted_iota(jnp.int32, shape, 1)
    row = lax.broadcasted_iota(jnp.int32, shape, 0)
    part = lambda t, q: (slice(k + t * PAN, k + (t + 1) * PAN), slice(q * BLK, (q + 1) * BLK))
    left = [work[part(t, home)] for t in range(tiles)]
    inside = (lane >= offset) & (lane < offset + SUB)
    right = []
    for t in range(tiles):
        unit = jnp.where(lane == row + (offset + t * PAN), 1.0, 0.0)
        right.append(
            [jnp.where(inside, unit, left[t]) if q == home else work[part(t, q)] for q in range(groups)]
        )
    spread = lambda value: jnp.broadcast_to(value, shape)
    lanes = lambda value, c: jnp.take_along_axis(value, jnp.full(shape, c, jnp.int32), axis=1)
    for m in range(tiles):
        c, more = offset + m * PAN, m + 1 < tiles
        here = range(m, tiles)
        cols = {t: [lanes(left[t], c + j) for j in range(PAN)] for t in here}
        grid = [[spread(cols[m][j][i : i + 1, :]) for i in range(j, PAN)] for j in range(PAN)]
        for j in range(PAN):
            scale = lax.rsqrt(grid[j][0])
            factor = {i: grid[j][i - j] * scale for i in range(j + 1, PAN)}
            for q in range(j + 1, PAN):
                grid[q] = [grid[q][i - q] - factor[i] * factor[q] for i in range(q, PAN)]
            head = {t: cols[t][j] * scale for t in here}
            below = jnp.where(row > j, head[m], 0.0)
            pivot = [spread(value[j : j + 1, :]) * scale for value in right[m]]
            right[m] = [
                jnp.where(row == j, p, value - below * p) for p, value in zip(pivot, right[m])
            ]
            if more:
                ahead = spread(left[m][j : j + 1, :]) * scale
                left[m] = left[m] - below * ahead
            for t in here[1:]:
                right[t] = [value - head[t] * p for p, value in zip(pivot, right[t])]
                left[t] = left[t] - head[t] * ahead
            for i in range(j + 1, PAN):
                for t in here:
                    cols[t][i] = cols[t][i] - factor[i] * head[t]
        for q in range(groups):
            work[part(m, q)] = right[m][q]
        for task in later[m::tiles]:
            task()


def split_rows(value, parts):
    for n in range(3):
        term = value.astype(jnp.bfloat16)
        parts[n * SUB : (n + 1) * SUB, :] = term
        value = value - term.astype(jnp.float32)


def product_terms(parts, block, other, span):
    term = lambda source, n, span: source[n * SUB : (n + 1) * SUB, span]
    turned = jnp.concatenate([term(parts, n, block) for n in (0, 1, 2, 0)], 0).T
    none = jnp.zeros((2 * SUB, span.stop - span.start), jnp.bfloat16)
    terms = [term(other, n, span) for n in (0, 0, 0, 1, 2, 1)] + [none]
    return turned, jnp.concatenate(terms, 0)


def update_block(work, parts, lower, i):
    rows = slice(i * BLK, (i + 1) * BLK)
    for span in (slice(0, BLK), slice(i * BLK, work.shape[1])):
        total = None
        for n in range(BLK // SUB):
            other = parts.at[n] if span.start else lower.at[n]
            turned, terms = product_terms(parts.at[n], rows, other, span)
            product = jnp.dot(
                jnp.concatenate([turned, turned], 1), terms, preferred_element_type=jnp.float32
            )
            total = product if total is None else total + product
        work[rows, span] = work[rows, span] - total if span.start else -total


def update_below(work, parts, k, first, last):
    size = work.shape[1]
    home, h = k // BLK, first // BLK
    rows, block = slice(first, last), slice(h * BLK, (h + 1) * BLK)
    for low, high in ((0, home + 1), (max(h, home + 1), size // BLK)):
        if low < high:
            span = slice(low * BLK, high * BLK)
            turned, terms = product_terms(parts, block, parts, span)
            turned = turned[first - h * BLK : last - h * BLK]
            old = work[rows, span]
            if low <= home < high:
                lane = lax.broadcasted_iota(jnp.int32, old.shape, 1) + low * BLK
                old = jnp.where((lane >= k) & (lane < k + SUB), 0.0, old)
            work[rows, span] = old - jnp.dot(
                jnp.concatenate([turned, turned], 1), terms, preferred_element_type=jnp.float32
            )


def factor_steps(count, packed_ref, out_ref, work, parts, lower, started=None, arrived=None):
    size = count * BLK

    def take(i):
        for j in range(i, count):
            work[i * BLK : (i + 1) * BLK, j * BLK : (j + 1) * BLK] = packed_ref[place(i, j, count)]

    take(0)
    later = []
    for k in range(0, size, SUB):
        n, last = k // SUB, BLK if k < BLK else size
        eliminate(work, k, later)
        rows = work[k : k + SUB, :]
        if k + SUB < size:
            split_rows(rows, parts.at[n])
        if k + SUB < last:
            update_below(work, parts.at[n], k, k + SUB, k + 2 * SUB)
        starts = [k + 2 * SUB, *range((k + 2 * SUB) // BLK * BLK + BLK, last, BLK)]
        later = [
            functools.partial(update_below, work, parts.at[n], k, first, first // BLK * BLK + BLK)
            for first in starts
            if first < last
        ]
        if k < BLK:
            lane = lax.broadcasted_iota(jnp.int32, (SUB, BLK), 1)
            split_rows(jnp.where(lane < k + SUB, rows[:, :BLK], 0.0), lower.at[n])
        if k == 0 and started:
            started()
        if k + SUB == BLK:
            if arrived:
                arrived()
            for i in range(1, count):
                take(i)
                update_block(work, parts, lower, i)
    for k in range(0, size, SUB):
        lane = lax.broadcasted_iota(jnp.int32, (SUB, size), 1)
        kept = jnp.where(lane < k + SUB, work[k : k + SUB, :], 0.0)
        out_ref[k : k + SUB, :] = kept.astype(out_ref.dtype)


def inverse_factor(packed):
    size = packed.shape[0] * 2
    count = size // BLK
    vmem = pl.BlockSpec(memory_space=pltpu.VMEM)
    return pl.pallas_call(
        functools.partial(factor_steps, count),
        out_shape=jax.ShapeDtypeStruct((size, size), jnp.bfloat16),
        in_specs=[vmem],
        out_specs=vmem,
        scratch_shapes=[
            pltpu.VMEM((size, size), jnp.float32),
            pltpu.VMEM((size // SUB, 3 * SUB, size), jnp.bfloat16),
            pltpu.VMEM((BLK // SUB, 3 * SUB, BLK), jnp.bfloat16),
        ],
    )(packed)


def shards(wavefunctions, stiffness, cell_scale, potential):
    if fits(*wavefunctions.shape, lax.axis_size("band"), lax.axis_size("cell")):
        slices, own, ahead, middle, inverse = filtered(
            wavefunctions, stiffness, cell_scale, potential
        )
        return rotated_here(inverse, slices, own, ahead, middle)
    anchor = wavefunctions.astype(jnp.float32)
    degree_one = (
        (apply_h(wavefunctions, stiffness, cell_scale, potential) - centre * anchor) / half_width
    ).astype(jnp.bfloat16)
    one_wide = degree_one.astype(jnp.float32)
    degree_two = (
        2.0
        * (apply_h(degree_one, stiffness, cell_scale, potential) - centre * one_wide)
        / half_width
        - anchor
    ).astype(jnp.bfloat16)
    two_wide = degree_two.astype(jnp.float32)
    degree_three = (
        2.0
        * (apply_h(degree_two, stiffness, cell_scale, potential) - centre * two_wide)
        / half_width
        - one_wide
    ).astype(jnp.bfloat16)
    slices = lax.all_to_all(degree_three, "band", split_axis=1, concat_axis=0, tiled=True)
    inverse = inverse_factor(margin_packed(slices))
    rotated = jnp.dot(inverse, slices, preferred_element_type=jnp.float32).astype(jnp.bfloat16)
    return lax.all_to_all(rotated, "band", split_axis=0, concat_axis=1, tiled=True)


def solution(mesh):
    in_specs = (P("band", "cell"), P(), P("cell"), P("cell", None))
    out_specs = P("band", "cell")
    return jax.shard_map(shards, mesh=mesh, in_specs=in_specs, out_specs=out_specs, check_vma=False)
```

```python
import functools
import jax
import jax.numpy as jnp
from jax import lax
from jax.experimental import pallas as pl
from jax.experimental.pallas import tpu as pltpu
from jax.sharding import PartitionSpec as P

PLANE = 64
OWN = 448
BLK = 128
PAN = 8
SUB = 32
EARLY = 1
MIDDLE = 3
MESH = pl.DeviceIdType.MESH

centre = 4.0
half_width = 3.0


def shifted(block, axis, distance):
    devices = range(lax.axis_size(axis))
    route = [((i - distance) % len(devices), i) for i in devices]
    return lax.ppermute(block, axis, route)


def apply_h(field, stiffness, cell_scale, potential):
    band_rows = field.shape[0]
    cell_count = field.shape[1] // OWN
    following = shifted(field[:, :PLANE], "cell", -1)
    owned_part = field.reshape(band_rows, cell_count, OWN)
    top_plane = jnp.concatenate([owned_part[:, 1:, :PLANE], following[:, None, :]], 1)
    cell_nodes = jnp.concatenate([owned_part, top_plane], 2)
    stiff_part = jnp.einsum(
        "bcn,nm->bcm", cell_nodes, stiffness, preferred_element_type=jnp.float32
    )
    cell_result = cell_scale[None, :, None] * stiff_part + potential[None] * cell_nodes.astype(
        jnp.float32
    )
    spill = cell_result[:, :, OWN:]
    incoming = shifted(spill[:, -1], "cell", 1)
    spill = jnp.concatenate([incoming[:, None, :], spill[:, :-1]], 1)
    kept = cell_result[:, :, :OWN]
    kept = jnp.concatenate([kept[:, :, :PLANE] + spill, kept[:, :, PLANE:]], 2)
    return kept.reshape(band_rows, cell_count * OWN)


def place(i, j, count):
    tall = count // 2
    n = j if i == 0 else count + (j - i) + sum(count - m for m in range(1, i))
    return slice(n % tall * BLK, (n % tall + 1) * BLK), slice(n // tall * BLK, (n // tall + 1) * BLK)


def pack(packed_ref, row_of_blocks, i, count):
    for j in range(i, count):
        packed_ref[place(i, j, count)] = row_of_blocks[:, (j - i) * BLK : (j - i + 1) * BLK]


def packed_gram(slices_ref, packed_ref, count):
    for i in range(count):
        product = lax.dot_general(
            slices_ref[i * BLK : (i + 1) * BLK, :],
            slices_ref[i * BLK :, :],
            (((1,), (1,)), ((), ())),
            preferred_element_type=jnp.float32,
        )
        pack(packed_ref, product, i, count)


def gram_kernel(count, slices_ref, packed_ref):
    packed_gram(slices_ref, packed_ref, count)


def rows_at(start, size):
    return pl.ds(pl.multiple_of(start, 8), size)


def pair_step(e, degree, source, older, target, st, potb, potx, shift=0, both_cells=True):
    at = lambda c, skip, size: pl.ds(pl.multiple_of(c * OWN + skip, 16), size)
    nodes = OWN + PLANE
    va, vb = source[at(e, 0, nodes), :], source[at(e + 1, 0, nodes), :]
    vp = source[at(e - 1, 0, nodes), :]
    both = jnp.dot(st[...], jnp.concatenate([va, vb], 1), preferred_element_type=jnp.float32)
    before = jnp.dot(st[OWN:nodes, :], vp, preferred_element_type=jnp.float32)
    scale = lambda c: potx[c][:, nodes:]
    wa, wb = va.astype(jnp.float32), vb.astype(jnp.float32)
    ya = scale(e) * both[:, :BLK] + potb[e] * wa
    yb = scale(e + 1) * both[:, BLK:] + potb[e + 1] * wb
    yp = scale(e - 1) * before + potb[e - 1, OWN:, :] * vp[OWN:].astype(jnp.float32)

    def finish(c, h, w, skip):
        size = h.shape[0]
        value = h - centre * w
        if degree == 1:
            value = value * (1.0 / half_width)
        else:
            value = value * (2.0 / half_width) - older[at(c, skip, size), :].astype(jnp.float32)
        target[at(c - shift, skip, size), :] = value.astype(target.dtype)

    if both_cells:
        finish(e, ya[:PLANE] + yp, wa[:PLANE], 0)
        finish(e, ya[PLANE:OWN], wa[PLANE:OWN], PLANE)
    finish(e + 1, yb[:PLANE] + ya[OWN:], wb[:PLANE], 0)
    finish(e + 1, yb[PLANE:OWN], wb[PLANE:OWN], PLANE)


def ahead_plan(bands):
    far = lambda i, j: bin(i ^ j).count("1") if bands == 4 else int(i != j)
    turns = {}
    plan = []
    for b in range(1, bands):
        for h in range(b):
            for q in [*range(b), *range(b + 1, bands)]:
                source = min((h, q), key=lambda i: (far(i, b), i != q))
                plan.append((far(source, b), source, b, h, q))
    ordered = []
    for _, source, b, h, q in sorted(plan):
        for part in range(2):
            turn = turns.get((source, b), 0)
            turns[source, b] = turn + 1
            ordered.append((turn, source, b, h, q, part))
    return sorted(ordered)


def part_start(part, each, bands):
    return part * each + jnp.where(part >= bands // 2, 2 * OWN, 0) if isinstance(part, jax.Array) else (
        part * each + (2 * OWN if part >= bands // 2 else 0)
    )


class Ahead:
    def __init__(self, bands, band, cell, slices, own, target, send_sem, recv_sem):
        self.band, self.bands = band, bands
        self.cell, self.slices, self.own, self.target = cell, slices, own, target
        self.send_sem, self.recv_sem = send_sem, recv_sem
        self.started, self.plan = [], ahead_plan(bands)
        self.count = [0] * bands

    def copy(self, slot, b, h, q, part, held):
        each = self.target.shape[2]
        size = each // 2
        n = q - (q > b)
        span = pl.ds(part * size, size)
        start = part_start(q, each, self.bands) + part * size
        source = self.slices.at[h, span] if held else self.own.at[pl.ds(start, size)]
        return pltpu.make_async_remote_copy(
            src_ref=source, dst_ref=self.target.at[h, n, span],
            send_sem=self.send_sem.at[slot],
            recv_sem=self.recv_sem.at[(h * (self.bands - 1) + n) * 2 + part],
            device_id={"band": b, "cell": self.cell}, device_id_type=MESH,
        )

    def start(self, first, last):
        for turn, source, b, h, q, part in self.plan:
            if first <= turn < last:
                slot = self.count[source]
                self.count[source] += 1
                copy = self.copy(slot, b, h, q, part, source == q)

                @pl.when(self.band == source)
                def _():
                    copy.start()

                self.started.append((source, b, copy))

    def finish(self):
        for source, b, copy in self.started:

            @pl.when(self.band == source)
            def _():
                copy.wait_send()

            @pl.when(self.band == b)
            def _():
                copy.wait_recv()


def filter_kernel(
    count, bands, cells, held, total,
    wave_ref, stiff_ref, scale_ref, potential_ref, slices_out, own_out, ahead_ref, middle_out, inverse_ref,
    slices_ref, three, middle_ref,
    pots, turned, ext, one, two, st, potx, potb,
    mine, from_core, half, from_band, quarter, from_z, piece, out_ref, work, parts, lower,
    send_sem, recv_sem, ahead_send, ahead_recv, middle_send, middle_recv, out_sem,
):
    band = lax.axis_index("band")
    cell = lax.axis_index("cell")
    core = lax.rem(cell, 2)
    level = lax.div(cell, 2)
    levels = cells // 2
    rows_half = mine.shape[0] // 2
    rows_band = rows_half // bands
    rows_z = rows_band // levels
    nodes = OWN + PLANE
    owned = held * OWN

    other_core = {"band": band, "cell": cell + 1 - 2 * core}
    band_peer = lambda o: lax.rem(band + o, bands)
    z_peer = lambda o: lax.rem(level + o, levels)
    band_device = lambda o: {"band": band_peer(o), "cell": cell}
    z_device = lambda o: {"band": band, "cell": z_peer(o) * 2 + core}
    cell_device = lambda o: {"band": band, "cell": lax.rem(cell + o, cells)}

    barrier = pltpu.get_barrier_semaphore()
    for o in range(1, bands):
        pl.semaphore_signal(barrier, inc=1, device_id=band_device(o), device_id_type=MESH)
    for o in range(1, cells):
        pl.semaphore_signal(barrier, inc=1, device_id=cell_device(o), device_id_type=MESH)
    used = [0]

    def send(src, dst, device):
        slot = used[0]
        used[0] += 1
        copy = pltpu.make_async_remote_copy(
            src_ref=src, dst_ref=dst, send_sem=send_sem.at[slot], recv_sem=recv_sem.at[slot],
            device_id=device, device_id_type=MESH,
        )
        copy.start()
        return copy

    low, high = 3 * OWN, 2 * OWN + PLANE
    right, left = cell_device(1), cell_device(cells - 1)

    def turn(q):
        span = slice(q * BLK, (q + 1) * BLK)
        turned[span, :] = wave_ref[:, span].T

    strips = owned // BLK
    first, last = -(-high // BLK), (owned - low) // BLK
    for c in range(held):
        pots[c, :, :nodes] = potential_ref[c : c + 1, :]
        pots[c, :, nodes:] = jnp.broadcast_to(scale_ref[:, c : c + 1], (1, BLK))
    for q in range(last, strips):
        turn(q)
    pl.semaphore_wait(barrier, bands - 1 + cells - 1)
    halo = [
        send(pots.at[held - 3 : held], potx.at[0:3], right),
        send(pots.at[0:2], potx.at[held + 3 : held + 5], left),
        send(turned.at[owned - low : owned], ext.at[0:low], right),
    ]
    for q in range(first):
        turn(q)
    halo.append(send(turned.at[0:high], ext.at[low + owned : low + owned + high], left))
    for q in range(first, last):
        turn(q)
    potx[3 : held + 3] = pots[...]
    ext[low : low + owned, :] = turned[...]
    st[...] = stiff_ref[...].T

    def columns(c):
        line = potx[c]
        for q in range(nodes // BLK):
            part = jnp.broadcast_to(line[:, q * BLK : (q + 1) * BLK], (BLK, BLK))
            potb[c, q * BLK : (q + 1) * BLK, :] = part.T

    @pl.loop(3, held + 3)
    def _(c):
        columns(c)

    mid, side = 2 + held // 2, held // 2 - 1
    each, quarter_each = ahead_ref.shape[2], slices_ref.shape[1] - ahead_ref.shape[2]
    middle = (mid - 3) * OWN

    @pl.loop(0, 3)
    def _(p):
        pair_step(mid - 2 + 2 * p, 1, ext, None, one, st, potb, potx)

    @pl.loop(0, 2)
    def _(p):
        pair_step(mid - 1 + 2 * p, 2, one, ext, two, st, potb, potx)

    pair_step(mid, 3, two, one, three, st, potb, potx, 3)

    def middle_copy(source, b, whole):
        start, size = (middle, 2 * OWN) if whole else (middle + b * quarter_each, quarter_each)
        target = middle_ref.at[source] if whole else slices_ref.at[source, pl.ds(each, quarter_each)]
        return pltpu.make_async_remote_copy(
            src_ref=three.at[pl.ds(start, size)], dst_ref=target,
            send_sem=middle_send.at[b], recv_sem=middle_recv.at[source],
            device_id={"band": b, "cell": cell}, device_id_type=MESH,
        )

    for b in reversed(range(bands)):
        for whole in (True, False):

            @pl.when(band < b if whole else band > b)
            def _():
                middle_copy(band, b, whole).start()

    for copy in halo:
        copy.wait()
    for c in (0, 1, 2, held + 3, held + 4):
        columns(c)
    outer = -(-(mid - 3) // 2)

    @pl.loop(0, 2 * outer)
    def _(p):
        e = jnp.where(p < outer, 1 + 2 * p, held + 3 - 2 * (p - outer))
        pair_step(e, 1, ext, None, one, st, potb, potx)

    @pl.loop(0, 2 * outer)
    def _(p):
        e = jnp.where(p < outer, 2 + 2 * p, held + 2 - 2 * (p - outer))
        pair_step(e, 2, one, ext, two, st, potb, potx)

    base = used[0]
    used[0] += bands - 1
    swaps = []
    near = lax.div(band, bands // 2)
    for upper in (1 - near, near):
        start = 3 + upper * (side + 2)

        @pl.loop(0, side // 2)
        def _(p):
            pair_step(start + 2 * p, 3, two, one, three, st, potb, potx, 3)

        if side % 2:
            pair_step(start + side - 2, 3, two, one, three, st, potb, potx, 3, both_cells=False)
        for n in range(bands // 2):
            part = upper * (bands // 2) + n
            from_row = part_start(part, each, bands)
            for o in range(1, bands):

                @pl.when(band_peer(o) == part)
                def _():
                    pltpu.make_async_remote_copy(
                        src_ref=three.at[pl.ds(pl.multiple_of(from_row, 16), each)],
                        dst_ref=slices_ref.at[band, pl.ds(0, each)],
                        send_sem=send_sem.at[base + o - 1], recv_sem=recv_sem.at[base + o - 1],
                        device_id=band_device(o), device_id_type=MESH,
                    ).start()

    own_row = pl.multiple_of(part_start(band, each, bands), 16)
    slices_ref[band, pl.ds(0, each), :] = three[pl.ds(own_row, each), :]
    own_row = pl.multiple_of(middle + band * quarter_each, 16)
    slices_ref[band, pl.ds(each, quarter_each), :] = three[pl.ds(own_row, quarter_each), :]
    for o in range(1, bands):
        swaps.append(
            pltpu.make_async_remote_copy(
                src_ref=three.at[pl.ds(0, each)], dst_ref=slices_ref.at[band, pl.ds(0, each)],
                send_sem=send_sem.at[base + o - 1], recv_sem=recv_sem.at[base + o - 1],
                device_id=band_device(o), device_id_type=MESH,
            )
        )
    for h in range(bands):
        for whole in (True, False):

            @pl.when(band > h if whole else band < h)
            def _():
                middle_copy(h, 0, whole).wait_recv()
                if whole:
                    row = pl.multiple_of(band * quarter_each, 16)
                    slices_ref[h, pl.ds(each, quarter_each), :] = middle_ref[h, pl.ds(row, quarter_each), :]

    for copy in swaps:
        copy.wait()
    ahead = Ahead(bands, band, cell, slices_ref, three, ahead_ref, ahead_send, ahead_recv)
    ahead.start(0, EARLY)
    kept = [(slices_ref, slices_out), (three, own_out), (middle_ref, middle_out)]
    kept = [pltpu.make_async_copy(*pair, out_sem.at[n]) for n, pair in enumerate(kept)]
    for copy in kept:
        copy.start()

    for i in range(count):
        joined = jnp.concatenate([slices_ref[j] for j in range(i, count)], 1)
        product = jnp.dot(slices_ref[i].T, joined, preferred_element_type=jnp.float32)
        pack(mine, product, i, count)

    cuts = [0, 2 * BLK, (count + 1) * BLK]
    spans = [slice(cuts[n], cuts[n + 1]) for n in range(2)]
    start_half = core * rows_half
    start_band = start_half + band * rows_band
    start_z = start_band + level * rows_z

    def each_span(stage):
        return [stage(span) for span in spans]

    def wait_all(copies):
        for copy in copies:
            copy.wait()

    over_core = each_span(
        lambda span: [
            send(
                mine.at[rows_at((1 - core) * rows_half, rows_half), span],
                from_core.at[:, span],
                other_core,
            )
        ]
    )
    over_band = []
    for span, copies in zip(spans, over_core):
        wait_all(copies)
        half[:, span] = mine[rows_at(start_half, rows_half), span] + from_core[:, span]
        over_band.append([
            send(
                half.at[rows_at(band_peer(o) * rows_band, rows_band), span],
                from_band.at[o - 1, :, span],
                band_device(o),
            )
            for o in range(1, bands)
        ])
    over_z = []
    for span, copies in zip(spans, over_band):
        wait_all(copies)
        summed = half[rows_at(band * rows_band, rows_band), span]
        for o in range(1, bands):
            summed = summed + from_band[o - 1, :, span]
        quarter[:, span] = summed
        over_z.append([
            send(
                quarter.at[rows_at(z_peer(o) * rows_z, rows_z), span],
                from_z.at[o - 1, :, span],
                z_device(o),
            )
            for o in range(1, levels)
        ])
    ahead.start(EARLY, EARLY + MIDDLE)
    back_z = []
    for span, copies in zip(spans, over_z):
        wait_all(copies)
        summed = quarter[rows_at(level * rows_z, rows_z), span]
        for o in range(1, levels):
            summed = summed + from_z[o - 1, :, span]
        summed = summed / total
        piece[:, span] = summed
        here = rows_at(start_z, rows_z)
        out_ref[here, span] = summed
        back_z.append([
            send(piece.at[:, span], out_ref.at[here, span], z_device(o)) for o in range(1, levels)
        ])
    back_band = []
    for span, copies in zip(spans, back_z):
        wait_all(copies)
        here = out_ref.at[rows_at(start_band, rows_band), span]
        back_band.append([send(here, here, band_device(o)) for o in range(1, bands)])
    def to_core(n):
        wait_all(back_band[n])
        here = out_ref.at[rows_at(start_half, rows_half), spans[n]]
        return send(here, here, other_core)

    def rest_to_core():
        back_core.append(to_core(1))
        ahead.start(EARLY + MIDDLE, 1 << 10)

    back_core = [to_core(0)]
    back_core[0].wait()
    factor_steps(
        count, out_ref, inverse_ref, work, parts, lower, rest_to_core, lambda: back_core[1].wait()
    )
    ahead.finish()
    wait_all(kept)
    for b in range(bands):
        for whole in (True, False):

            @pl.when(band < b if whole else band > b)
            def _():
                middle_copy(band, b, whole).wait_send()


def filtered(wavefunctions, stiffness, cell_scale, potential):
    bands, cells = lax.axis_size("band"), lax.axis_size("cell")
    band_rows, owned = wavefunctions.shape
    held = owned // OWN
    nodes = OWN + PLANE
    count = band_rows * bands // BLK
    quarter_each = 2 * OWN // bands
    each = owned // bands - quarter_each
    total = float(owned * cells)
    height, width = count * BLK // 2, (count + 1) * BLK
    levels = cells // 2
    rows_half = height // 2
    rows_band = rows_half // bands
    rows_z = rows_band // levels
    sends = 4 + (bands - 1) + 4 * (1 + (bands - 1) + (levels - 1))
    size = count * BLK
    plan = ahead_plan(bands)
    departs = max(sum(copy[1] == b for copy in plan) for b in range(bands))
    spans = owned + 5 * OWN + PLANE
    vmem = pl.BlockSpec(memory_space=pltpu.VMEM)
    f32, bf16 = jnp.float32, jnp.bfloat16
    return pl.pallas_call(
        functools.partial(filter_kernel, count, bands, cells, held, total),
        out_shape=(
            jax.ShapeDtypeStruct((bands, each + quarter_each, BLK), bf16),
            jax.ShapeDtypeStruct((owned, BLK), bf16),
            jax.ShapeDtypeStruct((bands - 1, bands - 1, each, BLK), bf16),
            jax.ShapeDtypeStruct((bands - 1, 2 * OWN, BLK), bf16),
            jax.ShapeDtypeStruct((size, size), bf16),
        ),
        in_specs=[vmem] * 4,
        out_specs=(pl.BlockSpec(memory_space=pl.ANY),) * 4 + (vmem,),
        scratch_shapes=[
            pltpu.VMEM((bands, each + quarter_each, BLK), bf16),
            pltpu.VMEM((owned, BLK), bf16),
            pltpu.VMEM((bands - 1, 2 * OWN, BLK), bf16),
            pltpu.VMEM((held, 1, nodes + BLK), f32),
            pltpu.VMEM((owned, BLK), bf16),
            pltpu.VMEM((spans, BLK), bf16),
            pltpu.VMEM((spans, BLK), bf16),
            pltpu.VMEM((spans, BLK), bf16),
            pltpu.VMEM((nodes, nodes), bf16),
            pltpu.VMEM((held + 5, 1, nodes + BLK), f32),
            pltpu.VMEM((held + 5, nodes, BLK), f32),
            pltpu.VMEM((height, width), f32),
            pltpu.VMEM((rows_half, width), f32),
            pltpu.VMEM((rows_half, width), f32),
            pltpu.VMEM((bands - 1, rows_band, width), f32),
            pltpu.VMEM((rows_band, width), f32),
            pltpu.VMEM((levels - 1, rows_z, width), f32),
            pltpu.VMEM((rows_z, width), f32),
            pltpu.VMEM((height, width), f32),
            pltpu.VMEM((size, size), f32),
            pltpu.VMEM((size // SUB, 3 * SUB, size), bf16),
            pltpu.VMEM((BLK // SUB, 3 * SUB, BLK), bf16),
            pltpu.SemaphoreType.DMA((sends,)),
            pltpu.SemaphoreType.DMA((sends,)),
            pltpu.SemaphoreType.DMA((departs,)),
            pltpu.SemaphoreType.DMA((2 * (bands - 1) ** 2,)),
            pltpu.SemaphoreType.DMA((bands,)),
            pltpu.SemaphoreType.DMA((bands,)),
            pltpu.SemaphoreType.DMA((3,)),
        ],
        compiler_params=pltpu.CompilerParams(collective_id=0, has_side_effects=True),
    )(wavefunctions, stiffness, cell_scale[None, :], potential)


def rotate_kernel(bands, inverse_ref, slices_ref, own_ref, ahead_ref, middle_ref, out_ref):
    band = lax.axis_index("band")
    each = ahead_ref.shape[2]
    middle = bands // 2 * each
    edges = [(part_start(q, each, bands), q) for q in range(bands)] + [(middle, None)]

    def rows(g, h, first, last):
        found = []
        for start, q in sorted(edges, key=lambda edge: edge[0]):
            low, high = max(first, start), min(last, start + (2 * OWN if q is None else each))
            if low < high:
                span = slice(low - start, high - start)
                found.append(
                    middle_ref[h, span] if q is None else slices_ref[h, span] if q == g
                    else ahead_ref[h, q - (q > g), span]
                )
        return jnp.concatenate(found, 0)

    for g in range(bands):

        @pl.when(band == g)
        def _():
            some = inverse_ref[g * BLK : (g + 1) * BLK, : (g + 1) * BLK]
            for first in range(0, own_ref.shape[0], 2 * OWN):
                here = slice(first, first + 2 * OWN)
                joined = [rows(g, h, here.start, here.stop) for h in range(g)] + [own_ref[here, :]]
                out_ref[:, here] = lax.dot_general(
                    some, jnp.concatenate(joined, 1), (((1,), (1,)), ((), ())),
                    preferred_element_type=jnp.float32,
                ).astype(out_ref.dtype)


def rotated_here(inverse, slices, own, ahead, middle):
    bands = slices.shape[0]
    vmem = pl.BlockSpec(memory_space=pltpu.VMEM)
    return pl.pallas_call(
        functools.partial(rotate_kernel, bands),
        out_shape=jax.ShapeDtypeStruct(own.shape[::-1], own.dtype),
        in_specs=[vmem] * 5,
        out_specs=vmem,
    )(inverse, slices, own, ahead, middle)


def fits(band_rows, owned, bands, cells):
    height = band_rows * bands // 2
    return (
        band_rows == BLK
        and owned % OWN == 0
        and bands >= 3
        and bands % 2 == 0
        and cells % 2 == 0
        and cells >= 4
        and owned // OWN >= 8
        and owned // OWN % 2 == 0
        and 2 * OWN % (16 * bands) == 0
        and (owned - 2 * OWN) % (32 * bands) == 0
        and height % (16 * bands * (cells // 2)) == 0
    )


def margin_packed(slices):
    bands, cells = lax.axis_size("band"), lax.axis_size("cell")
    band_total, nodes = slices.shape
    count = band_total // BLK
    shape = jax.ShapeDtypeStruct((band_total // 2, (count + 1) * BLK), jnp.float32)
    vmem = pl.BlockSpec(memory_space=pltpu.VMEM)
    partial = pl.pallas_call(
        functools.partial(gram_kernel, count), out_shape=shape, in_specs=[vmem], out_specs=vmem
    )(slices)
    return lax.psum(partial, ("band", "cell")) / float(nodes * bands * cells)


def eliminate(work, k, later):
    groups, tiles = work.shape[1] // BLK, SUB // PAN
    home, offset = k // BLK, k % BLK
    shape = (PAN, BLK)
    lane = lax.broadcasted_iota(jnp.int32, shape, 1)
    row = lax.broadcasted_iota(jnp.int32, shape, 0)
    part = lambda t, q: (slice(k + t * PAN, k + (t + 1) * PAN), slice(q * BLK, (q + 1) * BLK))
    left = [work[part(t, home)] for t in range(tiles)]
    inside = (lane >= offset) & (lane < offset + SUB)
    right = []
    for t in range(tiles):
        unit = jnp.where(lane == row + (offset + t * PAN), 1.0, 0.0)
        right.append(
            [jnp.where(inside, unit, left[t]) if q == home else work[part(t, q)] for q in range(groups)]
        )
    spread = lambda value: jnp.broadcast_to(value, shape)
    lanes = lambda value, c: jnp.take_along_axis(value, jnp.full(shape, c, jnp.int32), axis=1)
    for m in range(tiles):
        c, more = offset + m * PAN, m + 1 < tiles
        here = range(m, tiles)
        cols = {t: [lanes(left[t], c + j) for j in range(PAN)] for t in here}
        grid = [[spread(cols[m][j][i : i + 1, :]) for i in range(j, PAN)] for j in range(PAN)]
        for j in range(PAN):
            scale = lax.rsqrt(grid[j][0])
            factor = {i: grid[j][i - j] * scale for i in range(j + 1, PAN)}
            for q in range(j + 1, PAN):
                grid[q] = [grid[q][i - q] - factor[i] * factor[q] for i in range(q, PAN)]
            head = {t: cols[t][j] * scale for t in here}
            below = jnp.where(row > j, head[m], 0.0)
            pivot = [spread(value[j : j + 1, :]) * scale for value in right[m]]
            right[m] = [
                jnp.where(row == j, p, value - below * p) for p, value in zip(pivot, right[m])
            ]
            if more:
                ahead = spread(left[m][j : j + 1, :]) * scale
                left[m] = left[m] - below * ahead
            for t in here[1:]:
                right[t] = [value - head[t] * p for p, value in zip(pivot, right[t])]
                left[t] = left[t] - head[t] * ahead
            for i in range(j + 1, PAN):
                for t in here:
                    cols[t][i] = cols[t][i] - factor[i] * head[t]
        for q in range(groups):
            work[part(m, q)] = right[m][q]
        for task in later[m::tiles]:
            task()


def split_rows(value, parts):
    for n in range(3):
        term = value.astype(jnp.bfloat16)
        parts[n * SUB : (n + 1) * SUB, :] = term
        value = value - term.astype(jnp.float32)


def product_terms(parts, block, other, span):
    term = lambda source, n, span: source[n * SUB : (n + 1) * SUB, span]
    turned = jnp.concatenate([term(parts, n, block) for n in (0, 1, 2, 0)], 0).T
    none = jnp.zeros((2 * SUB, span.stop - span.start), jnp.bfloat16)
    terms = [term(other, n, span) for n in (0, 0, 0, 1, 2, 1)] + [none]
    return turned, jnp.concatenate(terms, 0)


def update_block(work, parts, lower, i):
    rows = slice(i * BLK, (i + 1) * BLK)
    for span in (slice(0, BLK), slice(i * BLK, work.shape[1])):
        total = None
        for n in range(BLK // SUB):
            other = parts.at[n] if span.start else lower.at[n]
            turned, terms = product_terms(parts.at[n], rows, other, span)
            product = jnp.dot(
                jnp.concatenate([turned, turned], 1), terms, preferred_element_type=jnp.float32
            )
            total = product if total is None else total + product
        work[rows, span] = work[rows, span] - total if span.start else -total


def update_below(work, parts, k, first, last):
    size = work.shape[1]
    home, h = k // BLK, first // BLK
    rows, block = slice(first, last), slice(h * BLK, (h + 1) * BLK)
    for low, high in ((0, home + 1), (max(h, home + 1), size // BLK)):
        if low < high:
            span = slice(low * BLK, high * BLK)
            turned, terms = product_terms(parts, block, parts, span)
            turned = turned[first - h * BLK : last - h * BLK]
            old = work[rows, span]
            if low <= home < high:
                lane = lax.broadcasted_iota(jnp.int32, old.shape, 1) + low * BLK
                old = jnp.where((lane >= k) & (lane < k + SUB), 0.0, old)
            work[rows, span] = old - jnp.dot(
                jnp.concatenate([turned, turned], 1), terms, preferred_element_type=jnp.float32
            )


def factor_steps(count, packed_ref, out_ref, work, parts, lower, started=None, arrived=None):
    size = count * BLK

    def take(i):
        for j in range(i, count):
            work[i * BLK : (i + 1) * BLK, j * BLK : (j + 1) * BLK] = packed_ref[place(i, j, count)]

    take(0)
    later = []
    for k in range(0, size, SUB):
        n, last = k // SUB, BLK if k < BLK else size
        eliminate(work, k, later)
        rows = work[k : k + SUB, :]
        if k + SUB < size:
            split_rows(rows, parts.at[n])
        if k + SUB < last:
            update_below(work, parts.at[n], k, k + SUB, k + 2 * SUB)
        starts = [k + 2 * SUB, *range((k + 2 * SUB) // BLK * BLK + BLK, last, BLK)]
        later = [
            functools.partial(update_below, work, parts.at[n], k, first, first // BLK * BLK + BLK)
            for first in starts
            if first < last
        ]
        if k < BLK:
            lane = lax.broadcasted_iota(jnp.int32, (SUB, BLK), 1)
            split_rows(jnp.where(lane < k + SUB, rows[:, :BLK], 0.0), lower.at[n])
        if k == 0 and started:
            started()
        if k + SUB == BLK:
            if arrived:
                arrived()
            for i in range(1, count):
                take(i)
                update_block(work, parts, lower, i)
    for k in range(0, size, SUB):
        lane = lax.broadcasted_iota(jnp.int32, (SUB, size), 1)
        kept = jnp.where(lane < k + SUB, work[k : k + SUB, :], 0.0)
        out_ref[k : k + SUB, :] = kept.astype(out_ref.dtype)


def inverse_factor(packed):
    size = packed.shape[0] * 2
    count = size // BLK
    vmem = pl.BlockSpec(memory_space=pltpu.VMEM)
    return pl.pallas_call(
        functools.partial(factor_steps, count),
        out_shape=jax.ShapeDtypeStruct((size, size), jnp.bfloat16),
        in_specs=[vmem],
        out_specs=vmem,
        scratch_shapes=[
            pltpu.VMEM((size, size), jnp.float32),
            pltpu.VMEM((size // SUB, 3 * SUB, size), jnp.bfloat16),
            pltpu.VMEM((BLK // SUB, 3 * SUB, BLK), jnp.bfloat16),
        ],
    )(packed)


def shards(wavefunctions, stiffness, cell_scale, potential):
    if fits(*wavefunctions.shape, lax.axis_size("band"), lax.axis_size("cell")):
        slices, own, ahead, middle, inverse = filtered(
            wavefunctions, stiffness, cell_scale, potential
        )
        return rotated_here(inverse, slices, own, ahead, middle)
    anchor = wavefunctions.astype(jnp.float32)
    degree_one = (
        (apply_h(wavefunctions, stiffness, cell_scale, potential) - centre * anchor) / half_width
    ).astype(jnp.bfloat16)
    one_wide = degree_one.astype(jnp.float32)
    degree_two = (
        2.0
        * (apply_h(degree_one, stiffness, cell_scale, potential) - centre * one_wide)
        / half_width
        - anchor
    ).astype(jnp.bfloat16)
    two_wide = degree_two.astype(jnp.float32)
    degree_three = (
        2.0
        * (apply_h(degree_two, stiffness, cell_scale, potential) - centre * two_wide)
        / half_width
        - one_wide
    ).astype(jnp.bfloat16)
    slices = lax.all_to_all(degree_three, "band", split_axis=1, concat_axis=0, tiled=True)
    inverse = inverse_factor(margin_packed(slices))
    rotated = jnp.dot(inverse, slices, preferred_element_type=jnp.float32).astype(jnp.bfloat16)
    return lax.all_to_all(rotated, "band", split_axis=0, concat_axis=1, tiled=True)


def solution(mesh):
    in_specs = (P("band", "cell"), P(), P("cell"), P("cell", None))
    out_specs = P("band", "cell")
    return jax.shard_map(shards, mesh=mesh, in_specs=in_specs, out_specs=out_specs, check_vma=False)
```
